256 devices in a mesh: pair: 8 (over z), intg: 32 (over y, x, core).
Axes of the slice: x: 4, y: 4, z: 8, core: 2. Of those that a mesh axis runs over, the one named last changes fastest.
Arguments:
- amplitudes: bfloat16 [3072, 32768], P('pair', 'intg'), may hold values from -6 to 6
- integrals: bfloat16 [8192, 32768], P('pair', 'intg'), may hold values from -0.0625 to 0.0625
- sym_rows: int32 [64], P('pair'), may hold values from 0 to 3
- sym_cols: int32 [256], P('intg'), may hold values from 0 to 3
- mirror_rows: int32 [8192], replicated, may hold values from 0 to 8191, as said below
Outputs:
- residual: bfloat16 [3072, 8192], P('intg', 'pair')
The draws below stay inside these ranges and needn't reach their ends.
Inputs may be any that keep to these rules, and one draw needn't show every extreme that they name: `mirror_rows`: an involution without fixed points; it maps the rows of each 128-row tile onto all rows of one other tile.
All inputs are finite; a program needn't handle non-finite values.
Results may differ from the reference program's by a relative error of at most 0.001.
Values may be sent and summed in bfloat16 or wider, within the bound.
No kernel may reach another device: no remote copies, remote signals or barrier semaphores. Data moves between devices by JAX's collectives and lax.ppermute only.
A program may use at most 128 MiB of HBM per device.

```python
import math
import jax
import jax.numpy as jnp
from jax import lax

TILE = 128
NSYM = 4
IJ = 3072
AB = 8192
CD = 32768


def draw_mirror_rows(key, part):
    key_tiles = jax.random.fold_in(key, 11)
    key_rows = jax.random.fold_in(key, 23)
    count = AB // TILE
    order = jax.random.permutation(key_tiles, count).astype(jnp.int32)
    position = jnp.argsort(order, stable=True).astype(jnp.int32)
    partner = order[position ^ 1]
    leading = position % 2 == 0
    shuffle = jax.random.permutation(key_rows, TILE).astype(jnp.int32)
    inverse = jnp.argsort(shuffle, stable=True).astype(jnp.int32)
    inner = jnp.where(leading[:, None], shuffle[None, :], inverse[None, :])
    mapped = partner[:, None] * TILE + inner
    return mapped.reshape(AB).astype(jnp.int32)


def with_ends(result, rng, least, high):
    longest = result.shape.index(max(result.shape))
    spots = []
    for shift in (0, 1):
        where = [jax.random.randint(jax.random.fold_in(rng, axis), (), 0, length) for axis, length in enumerate(result.shape)]
        where[longest] = (where[longest] + shift) % result.shape[longest]
        spots.append(tuple(where))
    return result.at[spots[0]].set(least).at[spots[1]].set(high)


def block_levels(rng, shape, shards, least, top_value):
    def one(axis_at, parts):
        steps = jax.random.uniform(jax.random.fold_in(jax.random.fold_in(rng, 6), axis_at), (parts,), jnp.float32, least / len(shards), top_value / len(shards))
        return jnp.repeat(jnp.exp(steps), shape[axis_at] // parts).reshape((-1,) + (1,) * (len(shape) - axis_at - 1))

    gain = one(*shards[0])
    for cut in shards[1:]:
        gain = gain * one(*cut)
    return gain


def gaussian(rng, extent, spread, bound, pieces=(), kind=jnp.bfloat16):
    result = spread * jax.random.normal(rng, extent, jnp.float32)
    if pieces:
        result = result * block_levels(rng, extent, pieces, -0.22, 0.18)
    return jnp.clip(result, -bound, bound).astype(kind)


def setup_inputs(seed: int = 0) -> dict:
    seeds = jax.random.split(jax.random.key(seed), 6)
    return {
        "amplitudes": gaussian(seeds[0], (IJ, CD), 1.0, 6.0, ((0, 8), (1, 32))),
        "integrals": gaussian(seeds[1], (AB, CD), (CD // NSYM) ** -0.5, 0.0625, ((0, 8), (1, 32))),
        "sym_rows": with_ends(jax.random.randint(seeds[2], (AB // TILE,), 0, NSYM), jax.random.fold_in(seeds[2], 1), 0, NSYM - 1).astype(jnp.int32),
        "sym_cols": with_ends(jax.random.randint(seeds[3], (CD // TILE,), 0, NSYM), jax.random.fold_in(seeds[3], 1), 0, NSYM - 1).astype(jnp.int32),
        "mirror_rows": draw_mirror_rows(jax.random.fold_in(seeds[5], 71), 0),
    }


def reference(amplitudes, integrals, sym_rows, sym_cols, mirror_rows):
    col_block = math.gcd(CD, 4096)
    row_sym = jnp.repeat(sym_rows, TILE)
    col_sym = jnp.repeat(sym_cols, TILE)

    def add_block(index, total):
        start = (index * col_block).astype(jnp.int32)
        values = lax.dynamic_slice_in_dim(integrals, start, col_block, 1)
        labels = lax.dynamic_slice_in_dim(col_sym, start, col_block, 0)
        allowed = jnp.where(row_sym[:, None] == labels[None, :], values, jnp.zeros((), jnp.bfloat16))
        left = lax.dynamic_slice_in_dim(amplitudes, start, col_block, 1)
        return total + lax.dot_general(left, allowed, (((1,), (1,)), ((), ())), preferred_element_type=jnp.float32)

    ladder = lax.fori_loop(0, CD // col_block, add_block, jnp.zeros((IJ, AB), jnp.float32))
    mirrored = jnp.take(ladder, mirror_rows, axis=1)
    return (ladder - mirrored).astype(jnp.bfloat16)
```

```python
import functools

import jax
import jax.numpy as jnp
from jax import lax
from jax.experimental import pallas as pl
from jax.experimental.pallas import tpu as pltpu
from jax.sharding import Mesh, PartitionSpec as P


TILE = 128
SWAP = ((0, 1), (1, 0))


def shift(n, d):
    return [(i, (i + d) % n) for i in range(n)]


def scatter_ring(part, halves, join, axis):
    far_up, far_down = halves(part(2))
    from_up = lax.ppermute(far_up, axis, shift(4, 1))
    from_down = lax.ppermute(far_down, axis, shift(4, -1))
    up_a, up_b = halves(part(1))
    down_a, down_b = halves(part(3))
    up = lax.ppermute(join(up_a + from_up, up_b), axis, shift(4, 1))
    down = lax.ppermute(join(down_a, down_b + from_down), axis, shift(4, -1))
    return part(0) + up + down


def pick(array, index, axis):
    return lax.dynamic_index_in_dim(array, index, axis, keepdims=False)


def mirror_kernel(tile_ref, lane_ref, sum_ref, out_ref):
    rows = sum_ref.shape[1]

    def one(t, carry):
        twin = tile_ref[t]
        column = pl.multiple_of((t % 8) * TILE, TILE)
        twin_column = pl.multiple_of((twin % 8) * TILE, TILE)
        own = sum_ref[t // 8, :, pl.ds(column, TILE)]
        other = sum_ref[twin // 8, :, pl.ds(twin_column, TILE)]
        lanes = jnp.broadcast_to(lane_ref[pl.ds(t, 1), :], (rows, TILE))
        other = jnp.take_along_axis(other, lanes, axis=1)
        out_ref[t // 8, :, pl.ds(column, TILE)] = (own - other).astype(out_ref.dtype)
        return carry

    lax.fori_loop(0, 64, one, 0)


def antisymmetrize(sums, mirror_rows):
    tiles = mirror_rows.reshape(-1, TILE)
    twin = tiles[:, 0] // TILE
    lanes = tiles % TILE
    return pl.pallas_call(
        mirror_kernel,
        out_shape=jax.ShapeDtypeStruct(sums.shape, jnp.bfloat16),
        in_specs=[
            pl.BlockSpec(memory_space=pltpu.SMEM),
            pl.BlockSpec(memory_space=pltpu.VMEM),
            pl.BlockSpec(memory_space=pltpu.VMEM),
        ],
        out_specs=pl.BlockSpec(memory_space=pltpu.VMEM),
    )(twin, lanes, sums)


def shards(levels, a, v, sym_rows, sym_cols, mirror_rows):
    z, y, x, c = (lax.axis_index(n) for n in "zyxc")
    ab, k = v.shape
    row_sym = jnp.repeat(sym_rows, TILE)
    col_sym = jnp.repeat(sym_cols, TILE)

    rows = a.shape[0] // 4
    quads = a.reshape(2, 2, rows, k)
    keep = pick(quads, c, 1)
    other = lax.ppermute(pick(quads, 1 - c, 1), "c", SWAP)
    masked = jnp.where(row_sym[:, None] == col_sym[None, :], v, jnp.zeros((), v.dtype))
    masked = jnp.concatenate([masked, lax.ppermute(masked, "c", SWAP)], axis=1)

    chunks = 2
    size = rows // chunks
    done = []
    for j in range(chunks):
        full = jnp.zeros((levels, 2 * size, 2 * k), a.dtype)
        for h, source in enumerate((keep, other)):
            block = source[:, j * size : (j + 1) * size].reshape(2 * size, k)
            full = lax.dynamic_update_slice(full, block[None], (z, 0, h * k))
            ups = levels // 2 - h
            for step, count in ((1, ups), (-1, levels - 1 - ups)):
                moving = block
                for s in range(1, count + 1):
                    moving = lax.ppermute(moving, "z", shift(levels, step))
                    at = (z - s * step) % levels
                    full = lax.dynamic_update_slice(full, moving[None], (at, 0, h * k))
        partial = lax.dot_general(
            full.reshape(levels * 2 * size, 2 * k), masked, (((1,), (1,)), ((), ())),
            preferred_element_type=jnp.float32,
        ).reshape(4, 4, size, ab)
        half = size // 2
        lanes = lambda t: (t[:, : ab // 2], t[:, ab // 2 :])
        join_lanes = lambda p, q: jnp.concatenate([p, q], axis=1)
        blocks = lambda t: (t[:2], t[2:])
        join_blocks = lambda p, q: jnp.concatenate([p, q], axis=0)
        for at, outer, inner, dim in ((0, "x", "y", 1), (half, "y", "x", 0)):
            piece = partial[:, :, at : at + half]
            me_outer, me_inner = (x, y) if outer == "x" else (y, x)
            summed = scatter_ring(
                lambda o: pick(piece, (me_outer + o) % 4, dim), blocks, join_blocks, outer
            )
            done.append(
                scatter_ring(
                    lambda o: pick(summed, (me_inner + o) % 4, 0), lanes, join_lanes, inner
                )
            )
    sums = jnp.concatenate(done, axis=0)

    share = rows // levels
    spread = lax.all_to_all(sums.reshape(levels, share, ab), "z", 0, 0)
    padded = jnp.pad(spread, ((0, 0), (0, -share % 16), (0, 0)))
    result = antisymmetrize(padded, mirror_rows)[:, :share]
    return lax.all_to_all(result, "z", 0, 0).reshape(rows, ab)


def solution(mesh):
    levels = mesh.shape["pair"]
    grid = Mesh(mesh.devices.reshape(levels, 4, 4, 2), ("z", "y", "x", "c"))
    plane = ("y", "x", "c")
    return jax.shard_map(
        functools.partial(shards, levels),
        mesh=grid,
        in_specs=(P("z", plane), P("z", plane), P("z"), P(plane), P()),
        out_specs=P(plane, "z"),
        check_vma=False,
    )
```

```python
import functools

import jax
import jax.numpy as jnp
from jax import lax
from jax.experimental import pallas as pl
from jax.experimental.pallas import tpu as pltpu
from jax.sharding import Mesh, PartitionSpec as P


TILE = 128
SWAP = ((0, 1), (1, 0))


def shift(n, d):
    return [(i, (i + d) % n) for i in range(n)]


def fan(n, d):
    return [
        (2 * i + c, 2 * ((i + (d if c == 0 else -d)) % n) + c)
        for i in range(n)
        for c in range(2)
    ]


def pick(array, index, axis):
    return lax.dynamic_index_in_dim(array, index, axis, keepdims=False)


def scatter_ring(part, axis, way):
    forward = functools.partial(lax.ppermute, axis_name=(axis, "c"), perm=fan(4, 1))
    backward = functools.partial(lax.ppermute, axis_name=(axis, "c"), perm=fan(4, -1))
    far = forward(part(2))
    behind = backward(part(-way))
    ahead = forward(part(way) + far)
    return part(0) + behind + ahead


def mirror_kernel(tile_ref, lane_ref, sum_ref, out_ref):
    rows = sum_ref.shape[1]
    for t in range(64):
        twin = tile_ref[t]
        twin_column = pl.multiple_of((twin % 8) * TILE, TILE)
        own = sum_ref[t // 8, :, (t % 8) * TILE : (t % 8 + 1) * TILE]
        other = sum_ref[twin // 8, :, pl.ds(twin_column, TILE)]
        lanes = jnp.broadcast_to(lane_ref[t : t + 1, :], (rows, TILE))
        other = jnp.take_along_axis(other, lanes, axis=1)
        out_ref[t // 8, :, (t % 8) * TILE : (t % 8 + 1) * TILE] = (own - other).astype(out_ref.dtype)


def antisymmetrize(sums, mirror_rows):
    tiles = mirror_rows.reshape(-1, TILE)
    twin = tiles[:, 0] // TILE
    lanes = tiles % TILE
    return pl.pallas_call(
        mirror_kernel,
        out_shape=jax.ShapeDtypeStruct(sums.shape, jnp.bfloat16),
        in_specs=[
            pl.BlockSpec(memory_space=pltpu.SMEM),
            pl.BlockSpec(memory_space=pltpu.VMEM),
            pl.BlockSpec(memory_space=pltpu.VMEM),
        ],
        out_specs=pl.BlockSpec(memory_space=pltpu.VMEM),
    )(twin, lanes, sums)


def shards(levels, a, v, sym_rows, sym_cols, mirror_rows):
    z, y, x, c = (lax.axis_index(n) for n in "zyxc")
    way = 1 - 2 * c
    ab, k = v.shape
    row_sym = jnp.repeat(sym_rows, TILE)
    col_sym = jnp.repeat(sym_cols, TILE)

    rows = a.shape[0] // 4
    quads = a.reshape(2, 2, rows, k)
    keep = pick(quads, c, 1)
    other = lax.ppermute(pick(quads, 1 - c, 1), "c", SWAP)
    masked = jnp.where(row_sym[:, None] == col_sym[None, :], v, jnp.zeros((), v.dtype))
    masked = jnp.concatenate([masked, lax.ppermute(masked, "c", SWAP)], axis=1)

    def gather_rings(start, size):
        full = jnp.zeros((levels, 2 * size, 2 * k), a.dtype)
        for h, source in enumerate((keep, other)):
            block = source[:, start : start + size].reshape(2 * size, k)
            full = lax.dynamic_update_slice(full, block[None], (z, 0, h * k))
            ups = levels // 2 - h
            for step, count in ((1, ups), (-1, levels - 1 - ups)):
                moving = block
                for s in range(1, count + 1):
                    moving = lax.ppermute(moving, "z", shift(levels, step))
                    at = (z - s * step) % levels
                    full = lax.dynamic_update_slice(full, moving[None], (at, 0, h * k))
        return full

    def gather_offloaded(start, size):
        block = jnp.concatenate([keep[:, start : start + size], other[:, start : start + size]], axis=2)
        return lax.all_gather(block.reshape(2 * size, 2 * k), "z", axis=0)

    done = []
    for start, size, gather in ((0, 64, gather_rings), (64, 32, gather_offloaded)):
        full = gather(start, size)
        partial = lax.dot_general(
            full.reshape(levels * 2 * size, 2 * k), masked, (((1,), (1,)), ((), ())),
            preferred_element_type=jnp.float32,
        ).reshape(4, 4, size, ab)
        half = size // 2
        for at, outer, inner, dim in ((0, "x", "y", 1), (half, "y", "x", 0)):
            piece = partial[:, :, at : at + half]
            me_outer, me_inner = (x, y) if outer == "x" else (y, x)
            summed = scatter_ring(lambda o: pick(piece, (me_outer + o) % 4, dim), outer, way)
            done.append(scatter_ring(lambda o: pick(summed, (me_inner + o) % 4, 0), inner, way))
    sums = jnp.concatenate(done, axis=0)

    share = rows // levels
    spread = lax.all_to_all(sums.reshape(levels, share, ab), "z", 0, 0)
    result = antisymmetrize(spread, mirror_rows)
    return lax.all_to_all(result, "z", 0, 0).reshape(rows, ab)


def solution(mesh):
    levels = mesh.shape["pair"]
    grid = Mesh(mesh.devices.reshape(levels, 4, 4, 2), ("z", "y", "x", "c"))
    plane = ("y", "x", "c")
    return jax.shard_map(
        functools.partial(shards, levels),
        mesh=grid,
        in_specs=(P("z", plane), P("z", plane), P("z"), P(plane), P()),
        out_specs=P(plane, "z"),
        check_vma=False,
    )
```

```python
import functools

import jax
import jax.numpy as jnp
from jax import lax
from jax.experimental import pallas as pl
from jax.experimental.pallas import tpu as pltpu
from jax.sharding import Mesh, PartitionSpec as P


TILE = 128
SWAP = ((0, 1), (1, 0))


def shift(n, d):
    return [(i, (i + d) % n) for i in range(n)]


def cross(n, d):
    return [(2 * i + c, 2 * ((i + d) % n) + 1 - c) for i in range(n) for c in range(2)]


def pick(array, index, axis):
    return lax.dynamic_index_in_dim(array, index, axis, keepdims=False)


def scatter_ring(part, axis):
    far = part(2)
    half = far.shape[0] // 2
    from_up = lax.ppermute(far[:half], axis, shift(4, 1))
    from_down = lax.ppermute(far[half:], axis, shift(4, -1))
    up, down = part(1), part(3)
    up = lax.ppermute(jnp.concatenate([up[:half] + from_up, up[half:]]), axis, shift(4, 1))
    down = lax.ppermute(jnp.concatenate([down[:half], down[half:] + from_down]), axis, shift(4, -1))
    return part(0) + up + down


def mirror_kernel(tile_ref, lane_ref, sum_ref, out_ref):
    rows = sum_ref.shape[1]
    for t in range(64):
        twin = tile_ref[t]
        twin_column = pl.multiple_of((twin % 8) * TILE, TILE)
        own = sum_ref[t // 8, :, (t % 8) * TILE : (t % 8 + 1) * TILE]
        other = sum_ref[twin // 8, :, pl.ds(twin_column, TILE)]
        lanes = jnp.broadcast_to(lane_ref[t : t + 1, :], (rows, TILE))
        other = jnp.take_along_axis(other, lanes, axis=1)
        out_ref[t // 8, :, (t % 8) * TILE : (t % 8 + 1) * TILE] = (own - other).astype(out_ref.dtype)


def antisymmetrize(sums, mirror_rows):
    tiles = mirror_rows.reshape(-1, TILE)
    twin = tiles[:, 0] // TILE
    lanes = tiles % TILE
    return pl.pallas_call(
        mirror_kernel,
        out_shape=jax.ShapeDtypeStruct(sums.shape, jnp.bfloat16),
        in_specs=[
            pl.BlockSpec(memory_space=pltpu.SMEM),
            pl.BlockSpec(memory_space=pltpu.VMEM),
            pl.BlockSpec(memory_space=pltpu.VMEM),
        ],
        out_specs=pl.BlockSpec(memory_space=pltpu.VMEM),
    )(twin, lanes, sums)


def shards(levels, a, v, sym_rows, sym_cols, mirror_rows):
    z, y, x, c = (lax.axis_index(n) for n in "zyxc")
    ab, k = v.shape
    row_sym = jnp.repeat(sym_rows, TILE)
    col_sym = jnp.repeat(sym_cols, TILE)

    rows = a.shape[0] // 4
    size = rows // 2
    quads = a.reshape(2, 2, rows, k)
    mine, theirs = pick(quads, c, 1), pick(quads, 1 - c, 1)
    swapped = lax.ppermute(theirs, "c", SWAP)
    masked = jnp.where(row_sym[:, None] == col_sym[None, :], v, jnp.zeros((), v.dtype))
    masked = jnp.concatenate([masked, lax.ppermute(masked, "c", SWAP)], axis=1)

    def gather(j):
        cut = lambda t: t[:, j * size : (j + 1) * size].reshape(2 * size, k)
        columns = []
        for h in range(2):
            blocks = {0: cut(swapped if h else mine)}
            ups = levels // 2 - (h ^ j)
            for step, count in ((1, ups), (-1, levels - 1 - ups)):
                moving = cut(theirs if h else mine)
                for s in range(1, count + 1):
                    if h and s == 1:
                        moving = lax.ppermute(moving, ("z", "c"), cross(levels, step))
                    else:
                        moving = lax.ppermute(moving, "z", shift(levels, step))
                    blocks[-s * step % levels] = moving
            columns.append(jnp.concatenate([blocks[r] for r in range(levels)]))
        return jnp.concatenate(columns, axis=1)

    def product(j):
        return lax.dot_general(
            gather(j), masked, (((1,), (1,)), ((), ())), preferred_element_type=jnp.float32
        )

    first = product(0).reshape(4, 2, 2, size, ab)

    def parity(at):
        return (at // 2 - z) % 2

    def of_x(o):
        at = (x + o) % 4
        piece = lax.dynamic_slice(first, (0, parity(at), at % 2, 0, 0), (4, 1, 1, size, ab))
        return piece.reshape(4, size, ab)

    summed = scatter_ring(of_x, "x")
    turn = (x // 2 - z - parity(x)) // 2
    first = scatter_ring(lambda o: pick(summed, (y + o + turn) % 4, 0), "y")

    second = product(1).reshape(levels, 2, size, ab)

    def of_y(o):
        at = 2 * (y + o) - z
        return jnp.concatenate([pick(second, (at + i) % levels, 0) for i in range(2)])

    summed_y = scatter_ring(of_y, "y")
    second = scatter_ring(lambda o: pick(summed_y, (x + o) % 4, 0), "x")
    sums = jnp.concatenate([first, second], axis=0)

    share = rows // levels
    spread = lax.all_to_all(sums.reshape(levels, share, ab), "z", 0, 0)
    result = antisymmetrize(spread, mirror_rows)
    return lax.all_to_all(result, "z", 0, 0).reshape(rows, ab)


def solution(mesh):
    levels = mesh.shape["pair"]
    grid = Mesh(mesh.devices.reshape(levels, 4, 4, 2), ("z", "y", "x", "c"))
    plane = ("y", "x", "c")
    return jax.shard_map(
        functools.partial(shards, levels),
        mesh=grid,
        in_specs=(P("z", plane), P("z", plane), P("z"), P(plane), P()),
        out_specs=P(plane, "z"),
        check_vma=False,
    )
```

```python
import functools

import jax
import jax.numpy as jnp
from jax import lax
from jax.experimental import pallas as pl
from jax.experimental.pallas import tpu as pltpu
from jax.sharding import Mesh, PartitionSpec as P


TILE = 128
SWAP = ((0, 1), (1, 0))


def shift(n, d):
    return [(i, (i + d) % n) for i in range(n)]


def cross(n, d):
    return [(2 * i + c, 2 * ((i + d) % n) + 1 - c) for i in range(n) for c in range(2)]


def pick(array, index, axis):
    return lax.dynamic_index_in_dim(array, index, axis, keepdims=False)


def scatter_ring(part, axis):
    far = part(2)
    half = far.shape[0] // 2
    from_up = lax.ppermute(far[:half], axis, shift(4, 1))
    from_down = lax.ppermute(far[half:], axis, shift(4, -1))
    up, down = part(1), part(3)
    up = lax.ppermute(jnp.concatenate([up[:half] + from_up, up[half:]]), axis, shift(4, 1))
    down = lax.ppermute(jnp.concatenate([down[:half], down[half:] + from_down]), axis, shift(4, -1))
    return part(0) + up + down


def product_kernel(start, size, *refs):
    *blocks, v_ref, out_ref, a_ref = refs
    levels = len(blocks) // 2
    rows, k = blocks[0].shape
    for i, block in enumerate(blocks):
        h, r = divmod(i, levels)
        for pair in range(2):
            into, of = (2 * r + pair) * size, pair * rows // 2 + start
            a_ref[into : into + size, h * k : (h + 1) * k] = block[of : of + size, :]
    wide, tall = 256, 256

    def column(n, carry):
        at = pl.ds(pl.multiple_of(n * wide, wide), wide)

        def row(m, carry):
            into = pl.ds(pl.multiple_of(m * tall, tall), tall)
            out_ref[into, at] = lax.dot_general(
                a_ref[into, :], v_ref[at, :], (((1,), (1,)), ((), ())),
                preferred_element_type=jnp.float32,
            )
            return carry

        return lax.fori_loop(0, a_ref.shape[0] // tall, row, carry)

    lax.fori_loop(0, v_ref.shape[0] // wide, column, 0)


def product(blocks, v, start, size):
    k, ab = blocks[0].shape[1], v.shape[0]
    total = len(blocks) * size
    vmem = pl.BlockSpec(memory_space=pltpu.VMEM)
    return pl.pallas_call(
        functools.partial(product_kernel, start, size),
        out_shape=jax.ShapeDtypeStruct((total, ab), jnp.float32),
        in_specs=[vmem] * (len(blocks) + 1),
        out_specs=vmem,
        scratch_shapes=[pltpu.VMEM((total, 2 * k), v.dtype)],
        cost_estimate=pl.CostEstimate(
            flops=4 * total * ab * k, bytes_accessed=4 * total * k + 4 * ab * k + 4 * total * ab, transcendentals=0
        ),
    )(*blocks, v)


def mirror_kernel(tile_ref, lane_ref, sum_ref, out_ref):
    rows = sum_ref.shape[1]
    for t in range(64):
        twin = tile_ref[t]
        twin_column = pl.multiple_of((twin % 8) * TILE, TILE)
        own = sum_ref[t // 8, :, (t % 8) * TILE : (t % 8 + 1) * TILE]
        other = sum_ref[twin // 8, :, pl.ds(twin_column, TILE)]
        lanes = jnp.broadcast_to(lane_ref[t : t + 1, :], (rows, TILE))
        other = jnp.take_along_axis(other, lanes, axis=1)
        out_ref[t // 8, :, (t % 8) * TILE : (t % 8 + 1) * TILE] = (own - other).astype(out_ref.dtype)


def antisymmetrize(sums, mirror_rows):
    tiles = mirror_rows.reshape(-1, TILE)
    twin = tiles[:, 0] // TILE
    lanes = tiles % TILE
    return pl.pallas_call(
        mirror_kernel,
        out_shape=jax.ShapeDtypeStruct(sums.shape, jnp.bfloat16),
        in_specs=[
            pl.BlockSpec(memory_space=pltpu.SMEM),
            pl.BlockSpec(memory_space=pltpu.VMEM),
            pl.BlockSpec(memory_space=pltpu.VMEM),
        ],
        out_specs=pl.BlockSpec(memory_space=pltpu.VMEM),
    )(twin, lanes, sums)


def shards(levels, a, v, sym_rows, sym_cols, mirror_rows):
    z, y, x, c = (lax.axis_index(n) for n in "zyxc")
    ab, k = v.shape
    row_sym = jnp.repeat(sym_rows, TILE)
    col_sym = jnp.repeat(sym_cols, TILE)

    rows = a.shape[0] // 4
    size = rows // 2
    quads = a.reshape(2, 2, rows, k)
    mine, theirs = pick(quads, c, 1), pick(quads, 1 - c, 1)
    swapped = lax.ppermute(theirs, "c", SWAP)
    masked = jnp.where(row_sym[:, None] == col_sym[None, :], v, jnp.zeros((), v.dtype))
    masked = jnp.concatenate([masked, lax.ppermute(masked, "c", SWAP)], axis=1)

    blocks = []
    for h in range(2):
        by_level = {0: (swapped if h else mine).reshape(2 * rows, k)}
        ups = levels // 2 - h
        for step, count in ((1, ups), (-1, levels - 1 - ups)):
            moving = (theirs if h else mine).reshape(2 * rows, k)
            for s in range(1, count + 1):
                if h and s == 1:
                    moving = lax.ppermute(moving, ("z", "c"), cross(levels, step))
                else:
                    moving = lax.ppermute(moving, "z", shift(levels, step))
                by_level[-s * step % levels] = moving
        blocks += [by_level[r] for r in range(levels)]

    first = product(blocks, masked, 0, size).reshape(4, 2, 2, size, ab)

    def parity(at):
        return (at // 2 - z) % 2

    def of_x(o):
        at = (x + o) % 4
        piece = lax.dynamic_slice(first, (0, parity(at), at % 2, 0, 0), (4, 1, 1, size, ab))
        return piece.reshape(4, size, ab)

    summed = scatter_ring(of_x, "x")
    turn = (x // 2 - z - parity(x)) // 2
    first = scatter_ring(lambda o: pick(summed, (y + o + turn) % 4, 0), "y")

    second = product(blocks, masked, size, size).reshape(levels, 2, size, ab)

    def of_y(o):
        at = 2 * (y + o) - z
        return jnp.concatenate([pick(second, (at + i) % levels, 0) for i in range(2)])

    summed_y = scatter_ring(of_y, "y")
    second = scatter_ring(lambda o: pick(summed_y, (x + o) % 4, 0), "x")
    sums = jnp.concatenate([first, second], axis=0)

    share = rows // levels
    spread = lax.all_to_all(sums.reshape(levels, share, ab), "z", 0, 0)
    result = antisymmetrize(spread, mirror_rows)
    return lax.all_to_all(result, "z", 0, 0).reshape(rows, ab)


def solution(mesh):
    levels = mesh.shape["pair"]
    grid = Mesh(mesh.devices.reshape(levels, 4, 4, 2), ("z", "y", "x", "c"))
    plane = ("y", "x", "c")
    return jax.shard_map(
        functools.partial(shards, levels),
        mesh=grid,
        in_specs=(P("z", plane), P("z", plane), P("z"), P(plane), P()),
        out_specs=P(plane, "z"),
        check_vma=False,
    )
```

```python
import functools

import jax
import jax.numpy as jnp
from jax import lax
from jax.experimental import pallas as pl
from jax.experimental.pallas import tpu as pltpu
from jax.sharding import Mesh, PartitionSpec as P


TILE = 128
SWAP = ((0, 1), (1, 0))


def shift(n, d):
    return [(i, (i + d) % n) for i in range(n)]


def cross(n, d):
    return [(2 * i + c, 2 * ((i + d) % n) + 1 - c) for i in range(n) for c in range(2)]


def pick(array, index, axis):
    return lax.dynamic_index_in_dim(array, index, axis, keepdims=False)


def scatter_ring(part, axis):
    far = part(2)
    half = far.shape[0] // 2
    from_up = lax.ppermute(far[:half], axis, shift(4, 1))
    from_down = lax.ppermute(far[half:], axis, shift(4, -1))
    up, down = part(1), part(3)
    up = lax.ppermute(jnp.concatenate([up[:half] + from_up, up[half:]]), axis, shift(4, 1))
    down = lax.ppermute(jnp.concatenate([down[:half], down[half:] + from_down]), axis, shift(4, -1))
    return part(0) + up + down


def product_kernel(size, *refs):
    own_ref, other_ref, *v_refs, _, _, first_ref, second_ref, a_ref = refs
    rows, k = own_ref.shape
    for h, block in enumerate((own_ref, other_ref)):
        for part in range(2):
            for pair in range(2):
                into, of = (2 * part + pair) * size, pair * rows // 2 + part * size
                a_ref[into : into + size, h * k : (h + 1) * k] = block[of : of + size, :]
    wide = 256

    def column(n, carry):
        at = pl.ds(pl.multiple_of(n * wide, wide), wide)
        sums = sum(
            lax.dot_general(
                a_ref[:, h * k : (h + 1) * k], v_ref[at, :], (((1,), (1,)), ((), ())),
                preferred_element_type=jnp.float32,
            )
            for h, v_ref in enumerate(v_refs)
        )
        first_ref[0, :, at] = sums[: 2 * size]
        second_ref[0, :, at] = sums[2 * size :]
        return carry

    lax.fori_loop(0, v_refs[0].shape[0] // wide, column, 0)


def product(own, other, v, level, levels, sums):
    rows, k = own.shape
    size, ab = rows // 4, v[0].shape[0]
    whole = lambda t: pl.BlockSpec(t.shape, lambda i: (0, 0))
    place = pl.BlockSpec((1, 2 * size, ab), lambda i: (level, 0, 0))
    return pl.pallas_call(
        functools.partial(product_kernel, size),
        grid=(1,),
        out_shape=[jax.ShapeDtypeStruct((levels, 2 * size, ab), jnp.float32)] * 2,
        in_specs=[whole(t) for t in (own, other, *v)] + [pl.BlockSpec(memory_space=pl.ANY)] * 2,
        out_specs=[place] * 2,
        scratch_shapes=[pltpu.VMEM((rows, 2 * k), own.dtype)],
        input_output_aliases={4: 0, 5: 1},
        cost_estimate=pl.CostEstimate(
            flops=4 * rows * ab * k, bytes_accessed=4 * rows * k + 4 * ab * k + 4 * rows * ab, transcendentals=0
        ),
    )(own, other, *v, *sums)


def mirror_kernel(tile_ref, lane_ref, sum_ref, out_ref):
    rows = sum_ref.shape[1]
    for t in range(64):
        twin = tile_ref[t]
        twin_column = pl.multiple_of((twin % 8) * TILE, TILE)
        own = sum_ref[t // 8, :, (t % 8) * TILE : (t % 8 + 1) * TILE]
        other = sum_ref[twin // 8, :, pl.ds(twin_column, TILE)]
        lanes = jnp.broadcast_to(lane_ref[t : t + 1, :], (rows, TILE))
        other = jnp.take_along_axis(other, lanes, axis=1)
        out_ref[t // 8, :, (t % 8) * TILE : (t % 8 + 1) * TILE] = (own - other).astype(out_ref.dtype)


def antisymmetrize(sums, mirror_rows):
    tiles = mirror_rows.reshape(-1, TILE)
    twin = tiles[:, 0] // TILE
    lanes = tiles % TILE
    return pl.pallas_call(
        mirror_kernel,
        out_shape=jax.ShapeDtypeStruct(sums.shape, jnp.bfloat16),
        in_specs=[
            pl.BlockSpec(memory_space=pltpu.SMEM),
            pl.BlockSpec(memory_space=pltpu.VMEM),
            pl.BlockSpec(memory_space=pltpu.VMEM),
        ],
        out_specs=pl.BlockSpec(memory_space=pltpu.VMEM),
    )(twin, lanes, sums)


def shards(levels, a, v, sym_rows, sym_cols, mirror_rows):
    z, y, x, c = (lax.axis_index(n) for n in "zyxc")
    ab, k = v.shape
    row_sym = jnp.repeat(sym_rows, TILE)
    col_sym = jnp.repeat(sym_cols, TILE)

    rows = a.shape[0] // 4
    size = rows // 2
    quads = a.reshape(2, 2, rows, k)
    mine, theirs = pick(quads, c, 1), pick(quads, 1 - c, 1)
    swapped = lax.ppermute(theirs, "c", SWAP)
    masked = jnp.where(row_sym[:, None] == col_sym[None, :], v, jnp.zeros((), v.dtype))
    both = (masked, lax.ppermute(masked, "c", SWAP))

    middle = levels // 2
    at_home = [t.reshape(2 * rows, k) for t in (mine, theirs)]
    moving = {(h, d): at_home[h] for h in range(2) for d in (1, -1)}
    blocks = [{0: t.reshape(2 * rows, k)} for t in (mine, swapped)]
    sums = [jnp.zeros((levels, 2 * size, ab), jnp.float32) for _ in range(2)]
    ready = []
    for s in range(1, middle + 1):
        for h in range(2):
            ways = (1, -1) if s < middle else (1 - 2 * h,)
            if h:
                for r in ready:
                    sums = product(blocks[0][r], blocks[1][r], both, r, levels, sums)
                if ready:
                    held = lax.optimization_barrier((*sums, *(moving[1, d] for d in ways)))
                    sums, hold = list(held[:2]), held[2:]
                    moving.update({(1, d): t for d, t in zip(ways, hold)})
            for d in ways:
                if h and s == 1:
                    got = lax.ppermute(moving[h, d], ("z", "c"), cross(levels, d))
                else:
                    got = lax.ppermute(moving[h, d], "z", shift(levels, d))
                moving[h, d] = blocks[h][-s * d % levels] = got
        ready = [0] if s == 1 else [levels - s + 1, s - 1]
    for r in (*ready, middle):
        sums = product(blocks[0][r], blocks[1][r], both, r, levels, sums)

    first = sums[0].reshape(4, 2, 2, size, ab)

    def parity(at):
        return (at // 2 - z) % 2

    def of_x(o):
        at = (x + o) % 4
        piece = lax.dynamic_slice(first, (0, parity(at), at % 2, 0, 0), (4, 1, 1, size, ab))
        return piece.reshape(4, size, ab)

    summed = scatter_ring(of_x, "x")
    turn = (x // 2 - z - parity(x)) // 2
    first = scatter_ring(lambda o: pick(summed, (y + o + turn) % 4, 0), "y")

    second = sums[1].reshape(levels, 2, size, ab)

    def of_y(o):
        at = 2 * (y + o) - z
        return jnp.concatenate([pick(second, (at + i) % levels, 0) for i in range(2)])

    summed_y = scatter_ring(of_y, "y")
    second = scatter_ring(lambda o: pick(summed_y, (x + o) % 4, 0), "x")
    sums = jnp.concatenate([first, second], axis=0)

    share = rows // levels
    spread = lax.all_to_all(sums.reshape(levels, share, ab), "z", 0, 0)
    result = antisymmetrize(spread, mirror_rows)
    return lax.all_to_all(result, "z", 0, 0).reshape(rows, ab)


def solution(mesh):
    levels = mesh.shape["pair"]
    grid = Mesh(mesh.devices.reshape(levels, 4, 4, 2), ("z", "y", "x", "c"))
    plane = ("y", "x", "c")
    return jax.shard_map(
        functools.partial(shards, levels),
        mesh=grid,
        in_specs=(P("z", plane), P("z", plane), P("z"), P(plane), P()),
        out_specs=P(plane, "z"),
        check_vma=False,
    )
```

```python
import functools

import jax
import jax.numpy as jnp
from jax import lax
from jax.experimental import pallas as pl
from jax.experimental.pallas import tpu as pltpu
from jax.sharding import Mesh, PartitionSpec as P


TILE = 128
SWAP = ((0, 1), (1, 0))


def shift(n, d):
    return [(i, (i + d) % n) for i in range(n)]


def cross(n, d):
    return [(2 * i + c, 2 * ((i + d) % n) + 1 - c) for i in range(n) for c in range(2)]


def pick(array, index, axis):
    return lax.dynamic_index_in_dim(array, index, axis, keepdims=False)


def scatter_ring(part, axis):
    far = part(2)
    half = far.shape[0] // 2
    from_up = lax.ppermute(far[:half], axis, shift(4, 1))
    from_down = lax.ppermute(far[half:], axis, shift(4, -1))
    up, down = part(1), part(3)
    up = lax.ppermute(jnp.concatenate([up[:half] + from_up, up[half:]]), axis, shift(4, 1))
    down = lax.ppermute(jnp.concatenate([down[:half], down[half:] + from_down]), axis, shift(4, -1))
    return part(0) + up + down


def product_kernel(size, count, *refs):
    blocks, v_refs, out_refs, a_ref = refs[: 2 * count], refs[2 * count : 2 * count + 2], refs[-3:-1], refs[-1]
    rows, k = blocks[0].shape
    half = 2 * size * count
    for i, block in enumerate(blocks):
        level, h = divmod(i, 2)
        for part in range(2):
            for pair in range(2):
                into, of = part * half + (2 * level + pair) * size, pair * rows // 2 + part * size
                a_ref[into : into + size, h * k : (h + 1) * k] = block[of : of + size, :]
    wide = 512

    def column(n, carry):
        at = pl.ds(pl.multiple_of(n * wide, wide), wide)
        sums = sum(
            lax.dot_general(
                a_ref[:, h * k : (h + 1) * k], v_ref[at, :], (((1,), (1,)), ((), ())),
                preferred_element_type=jnp.float32,
            )
            for h, v_ref in enumerate(v_refs)
        )
        for part, out_ref in enumerate(out_refs):
            out_ref[:, :, at] = sums[part * half : (part + 1) * half].reshape(count, 2 * size, wide)
        return carry

    lax.fori_loop(0, v_refs[0].shape[0] // wide, column, 0)


def product(blocks, v, group, levels, sums):
    rows, k = blocks[0].shape
    count, size, ab = len(blocks) // 2, rows // 4, v[0].shape[0]
    vmem = pl.BlockSpec(memory_space=pltpu.VMEM)
    place = pl.BlockSpec((count, 2 * size, ab), lambda i: (group, 0, 0))
    n = len(blocks) + 2
    return pl.pallas_call(
        functools.partial(product_kernel, size, count),
        grid=(1,),
        out_shape=[jax.ShapeDtypeStruct((levels, 2 * size, ab), jnp.float32)] * 2,
        in_specs=[vmem] * n + [pl.BlockSpec(memory_space=pl.ANY)] * len(sums),
        out_specs=[place] * 2,
        scratch_shapes=[pltpu.VMEM((count * rows, 2 * k), v[0].dtype)],
        input_output_aliases={n + i: i for i in range(len(sums))},
        compiler_params=pltpu.CompilerParams(vmem_limit_bytes=28 << 20),
        cost_estimate=pl.CostEstimate(
            flops=4 * count * rows * ab * k,
            bytes_accessed=4 * count * rows * k + 4 * ab * k + 4 * count * rows * ab,
            transcendentals=0,
        ),
    )(*blocks, *v, *sums)


def mirror_kernel(tile_ref, lane_ref, sum_ref, out_ref):
    rows = sum_ref.shape[1]
    for t in range(64):
        twin = tile_ref[t]
        twin_column = pl.multiple_of((twin % 8) * TILE, TILE)
        own = sum_ref[t // 8, :, (t % 8) * TILE : (t % 8 + 1) * TILE]
        other = sum_ref[twin // 8, :, pl.ds(twin_column, TILE)]
        lanes = jnp.broadcast_to(lane_ref[t : t + 1, :], (rows, TILE))
        other = jnp.take_along_axis(other, lanes, axis=1)
        out_ref[t // 8, :, (t % 8) * TILE : (t % 8 + 1) * TILE] = (own - other).astype(out_ref.dtype)


def antisymmetrize(sums, mirror_rows):
    tiles = mirror_rows.reshape(-1, TILE)
    twin = tiles[:, 0] // TILE
    lanes = tiles % TILE
    return pl.pallas_call(
        mirror_kernel,
        out_shape=jax.ShapeDtypeStruct(sums.shape, jnp.bfloat16),
        in_specs=[
            pl.BlockSpec(memory_space=pltpu.SMEM),
            pl.BlockSpec(memory_space=pltpu.VMEM),
            pl.BlockSpec(memory_space=pltpu.VMEM),
        ],
        out_specs=pl.BlockSpec(memory_space=pltpu.VMEM),
    )(twin, lanes, sums)


def shards(levels, a, v, sym_rows, sym_cols, mirror_rows):
    z, y, x, c = (lax.axis_index(n) for n in "zyxc")
    ab, k = v.shape
    row_sym = jnp.repeat(sym_rows, TILE)
    col_sym = jnp.repeat(sym_cols, TILE)

    rows = a.shape[0] // 4
    size = rows // 2
    quads = a.reshape(2, 2, rows, k)
    mine, theirs = pick(quads, c, 1), pick(quads, 1 - c, 1)
    swapped = lax.ppermute(theirs, "c", SWAP)
    masked = jnp.where(row_sym[:, None] == col_sym[None, :], v, jnp.zeros((), v.dtype))
    both = (masked, lax.ppermute(masked, "c", SWAP))

    middle = levels // 2
    at_home = [t.reshape(2 * rows, k) for t in (mine, theirs)]
    moving = {(h, d): at_home[h] for h in range(2) for d in (1, -1)}
    blocks = [{0: t.reshape(2 * rows, k)} for t in (mine, swapped)]
    near = [r % levels for r in range(-2, 2)]
    far = [r % levels for r in range(2, levels - 2)]
    gathered = lambda group: [blocks[h][r] for r in group for h in range(2)]
    sums = ()
    for s in range(1, middle + 1):
        for h in range(2):
            ways = (1, -1) if s < middle else (1 - 2 * h,)
            if h and s == 3:
                sums = product(gathered(near), both, 0, levels, sums)
                *sums, up, down = lax.optimization_barrier((*sums, moving[1, 1], moving[1, -1]))
                moving[1, 1], moving[1, -1] = up, down
            for d in ways:
                if h and s == 1:
                    got = lax.ppermute(moving[h, d], ("z", "c"), cross(levels, d))
                else:
                    got = lax.ppermute(moving[h, d], "z", shift(levels, d))
                moving[h, d] = blocks[h][-s * d % levels] = got
    sums = product(gathered(far), both, 1, levels, sums)

    first = sums[0].reshape(4, 2, 2, size, ab)

    def parity(at):
        return (at // 2 - z) % 2

    def of_x(o):
        at = (x + o) % 4
        piece = lax.dynamic_slice(first, (0, parity(at), at % 2, 0, 0), (4, 1, 1, size, ab))
        return piece.reshape(4, size, ab)

    summed = scatter_ring(of_x, "x")
    turn = (x // 2 - z - parity(x)) // 2 + 1
    first = scatter_ring(lambda o: pick(summed, (y + o + turn) % 4, 0), "y")

    second = sums[1].reshape(levels, 2, size, ab)

    def of_y(o):
        at = 2 * (y + o) - z + 2
        return jnp.concatenate([pick(second, (at + i) % levels, 0) for i in range(2)])

    summed_y = scatter_ring(of_y, "y")
    second = scatter_ring(lambda o: pick(summed_y, (x + o) % 4, 0), "x")
    sums = jnp.concatenate([first, second], axis=0)

    share = rows // levels
    spread = lax.all_to_all(sums.reshape(levels, share, ab), "z", 0, 0)
    result = antisymmetrize(spread, mirror_rows)
    return lax.all_to_all(result, "z", 0, 0).reshape(rows, ab)


def solution(mesh):
    levels = mesh.shape["pair"]
    grid = Mesh(mesh.devices.reshape(levels, 4, 4, 2), ("z", "y", "x", "c"))
    plane = ("y", "x", "c")
    return jax.shard_map(
        functools.partial(shards, levels),
        mesh=grid,
        in_specs=(P("z", plane), P("z", plane), P("z"), P(plane), P()),
        out_specs=P(plane, "z"),
        check_vma=False,
    )
```

```python
import functools

import jax
import jax.numpy as jnp
from jax import lax
from jax.experimental import pallas as pl
from jax.experimental.pallas import tpu as pltpu
from jax.sharding import Mesh, PartitionSpec as P


TILE = 128
SWAP = ((0, 1), (1, 0))


def shift(n, d):
    return [(i, (i + d) % n) for i in range(n)]


def cross(n, d):
    return [(2 * i + c, 2 * ((i + d) % n) + 1 - c) for i in range(n) for c in range(2)]


def pick(array, index, axis):
    return lax.dynamic_index_in_dim(array, index, axis, keepdims=False)


def scatter_ring(part, axis):
    far = part(2)
    half = far.shape[0] // 2
    from_up = lax.ppermute(far[:half], axis, shift(4, 1))
    from_down = lax.ppermute(far[half:], axis, shift(4, -1))
    rest = [(0, 0)] * (far.ndim - 1)
    up = part(1) + jnp.pad(from_up, [(0, half), *rest])
    down = part(3) + jnp.pad(from_down, [(half, 0), *rest])
    up = lax.ppermute(up, axis, shift(4, 1))
    down = lax.ppermute(down, axis, shift(4, -1))
    return part(0) + up + down


def product_kernel(size, count, *refs):
    blocks, v_refs, out_refs, a_ref = refs[: 2 * count], refs[2 * count : 2 * count + 2], refs[-3:-1], refs[-1]
    rows, k = blocks[0].shape
    half = 2 * size * count
    for i, block in enumerate(blocks):
        level, h = divmod(i, 2)
        for part in range(2):
            for pair in range(2):
                into, of = part * half + (2 * level + pair) * size, pair * rows // 2 + part * size
                a_ref[into : into + size, h * k : (h + 1) * k] = block[of : of + size, :]
    wide = 512

    def column(n, carry):
        at = pl.ds(pl.multiple_of(n * wide, wide), wide)
        sums = sum(
            lax.dot_general(
                a_ref[:, h * k : (h + 1) * k], v_ref[at, :], (((1,), (1,)), ((), ())),
                preferred_element_type=jnp.float32,
            )
            for h, v_ref in enumerate(v_refs)
        )
        for part, out_ref in enumerate(out_refs):
            out_ref[:, :, at] = sums[part * half : (part + 1) * half].reshape(count, 2 * size, wide)
        return carry

    lax.fori_loop(0, v_refs[0].shape[0] // wide, column, 0)


def product(blocks, v, group, levels, sums):
    rows, k = blocks[0].shape
    count, size, ab = len(blocks) // 2, rows // 4, v[0].shape[0]
    vmem = pl.BlockSpec(memory_space=pltpu.VMEM)
    place = pl.BlockSpec((count, 2 * size, ab), lambda i: (group, 0, 0))
    n = len(blocks) + 2
    return pl.pallas_call(
        functools.partial(product_kernel, size, count),
        grid=(1,),
        out_shape=[jax.ShapeDtypeStruct((levels, 2 * size, ab), jnp.float32)] * 2,
        in_specs=[vmem] * n + [pl.BlockSpec(memory_space=pl.ANY)] * len(sums),
        out_specs=[place] * 2,
        scratch_shapes=[pltpu.VMEM((count * rows, 2 * k), v[0].dtype)],
        input_output_aliases={n + i: i for i in range(len(sums))},
        compiler_params=pltpu.CompilerParams(vmem_limit_bytes=28 << 20),
        cost_estimate=pl.CostEstimate(
            flops=4 * count * rows * ab * k,
            bytes_accessed=4 * count * rows * k + 4 * ab * k + 4 * count * rows * ab,
            transcendentals=0,
        ),
    )(*blocks, *v, *sums)


def mirror_kernel(tile_ref, lane_ref, sum_ref, out_ref):
    rows = sum_ref.shape[1]
    for t in range(64):
        twin = tile_ref[t]
        twin_column = pl.multiple_of((twin % 8) * TILE, TILE)
        own = sum_ref[t // 8, :, (t % 8) * TILE : (t % 8 + 1) * TILE]
        other = sum_ref[twin // 8, :, pl.ds(twin_column, TILE)]
        lanes = jnp.broadcast_to(lane_ref[t : t + 1, :], (rows, TILE))
        other = jnp.take_along_axis(other, lanes, axis=1)
        out_ref[t // 8, :, (t % 8) * TILE : (t % 8 + 1) * TILE] = (own - other).astype(out_ref.dtype)


def antisymmetrize(sums, mirror_rows):
    tiles = mirror_rows.reshape(-1, TILE)
    twin = tiles[:, 0] // TILE
    lanes = tiles % TILE
    return pl.pallas_call(
        mirror_kernel,
        out_shape=jax.ShapeDtypeStruct(sums.shape, jnp.bfloat16),
        in_specs=[
            pl.BlockSpec(memory_space=pltpu.SMEM),
            pl.BlockSpec(memory_space=pltpu.VMEM),
            pl.BlockSpec(memory_space=pltpu.VMEM),
        ],
        out_specs=pl.BlockSpec(memory_space=pltpu.VMEM),
    )(twin, lanes, sums)


def shards(levels, a, v, sym_rows, sym_cols, mirror_rows):
    z, y, x, c = (lax.axis_index(n) for n in "zyxc")
    ab, k = v.shape
    row_sym = jnp.repeat(sym_rows, TILE)
    col_sym = jnp.repeat(sym_cols, TILE)

    rows = a.shape[0] // 4
    size = rows // 2
    quads = a.reshape(2, 2, rows, k)
    mine, theirs = pick(quads, c, 1), pick(quads, 1 - c, 1)
    swapped = lax.ppermute(theirs, "c", SWAP)
    masked = jnp.where(row_sym[:, None] == col_sym[None, :], v, jnp.zeros((), v.dtype))
    both = (masked, lax.ppermute(masked, "c", SWAP))

    middle = levels // 2
    at_home = [t.reshape(2 * rows, k) for t in (mine, theirs)]
    moving = {(h, d): at_home[h] for h in range(2) for d in (1, -1)}
    blocks = [{0: t.reshape(2 * rows, k)} for t in (mine, swapped)]
    near = [r % levels for r in range(-2, 2)]
    far = [r % levels for r in range(2, levels - 2)]
    gathered = lambda group: [blocks[h][r] for r in group for h in range(2)]
    sums = ()
    for s in range(1, middle + 1):
        for h in range(2):
            ways = (1, -1) if s < middle else (1 - 2 * h,)
            if h and s == 3:
                sums = product(gathered(near), both, 0, levels, sums)
            for d in ways:
                if h and s == 1:
                    got = lax.ppermute(moving[h, d], ("z", "c"), cross(levels, d))
                else:
                    got = lax.ppermute(moving[h, d], "z", shift(levels, d))
                moving[h, d] = blocks[h][-s * d % levels] = got
    sums = product(gathered(far), both, 1, levels, sums)

    first = sums[0].reshape(4, 2, 2, size, ab)

    def parity(at):
        return (at // 2 - z) % 2

    def of_x(o):
        at = (x + o) % 4
        piece = lax.dynamic_slice(first, (0, parity(at), at % 2, 0, 0), (4, 1, 1, size, ab))
        return piece.reshape(4, size, ab)

    summed = scatter_ring(of_x, "x")
    turn = (x // 2 - z - parity(x)) // 2 + 1
    first = scatter_ring(lambda o: pick(summed, (y + o + turn) % 4, 0), "y")

    second = sums[1].reshape(levels, 2, size, ab)

    def of_y(o):
        at = 2 * (y + o) - z + 2
        return jnp.concatenate([pick(second, (at + i) % levels, 0) for i in range(2)])

    summed_y = scatter_ring(of_y, "y")
    second = scatter_ring(lambda o: pick(summed_y, (x + o) % 4, 0), "x")
    sums = jnp.concatenate([first, second], axis=0)

    share = rows // levels
    spread = lax.all_to_all(sums.reshape(levels, share, ab), "z", 0, 0)
    result = antisymmetrize(spread, mirror_rows)
    return lax.all_to_all(result, "z", 0, 0).reshape(rows, ab)


def solution(mesh):
    levels = mesh.shape["pair"]
    grid = Mesh(mesh.devices.reshape(levels, 4, 4, 2), ("z", "y", "x", "c"))
    plane = ("y", "x", "c")
    return jax.shard_map(
        functools.partial(shards, levels),
        mesh=grid,
        in_specs=(P("z", plane), P("z", plane), P("z"), P(plane), P()),
        out_specs=P(plane, "z"),
        check_vma=False,
    )
```

```python
import functools

import jax
import jax.numpy as jnp
from jax import lax
from jax.experimental import pallas as pl
from jax.experimental.pallas import tpu as pltpu
from jax.sharding import Mesh, PartitionSpec as P


TILE = 128
SWAP = ((0, 1), (1, 0))


def shift(n, d):
    return [(i, (i + d) % n) for i in range(n)]


def cross(n, d):
    return [(2 * i + c, 2 * ((i + d) % n) + 1 - c) for i in range(n) for c in range(2)]


def pick(array, index, axis):
    return lax.dynamic_index_in_dim(array, index, axis, keepdims=False)


def scatter_ring(part, axis, early):
    far = part(2)
    half = far.shape[0] // 2
    rest = [(0, 0)] * (far.ndim - 1)
    send_up = functools.partial(lax.ppermute, axis_name=axis, perm=shift(4, 1))
    send_down = functools.partial(lax.ppermute, axis_name=axis, perm=shift(4, -1))
    from_up, from_down = send_up(far[:half]), send_down(far[half:])
    up, down = part(1), part(3)
    if not early:
        up = send_up(up + jnp.pad(from_up, [(0, half), *rest]))
        down = send_down(down + jnp.pad(from_down, [(half, 0), *rest]))
        return part(0) + up + down
    up_now, down_now = send_up(up[half:]), send_down(down[:half])
    up, down = send_up(up[:half] + from_up), send_down(down[half:] + from_down)
    return (
        part(0)
        + jnp.pad(up + down_now, [(0, half), *rest])
        + jnp.pad(down + up_now, [(half, 0), *rest])
    )


def product_kernel(size, count, *refs):
    blocks, given = refs[: 2 * count], refs[2 * count : 2 * count + 2]
    *out_refs, a_ref, v_own, v_other, sems = refs[-6:]
    v_refs = (v_own, v_other)
    rows, k = blocks[0].shape
    half = 2 * size * count
    copies = [pltpu.make_async_copy(src, dst, sems.at[i]) for i, (src, dst) in enumerate(zip(given, v_refs))]
    for i, block in enumerate(blocks):
        level, h = divmod(i, 2)
        for part in range(2):
            for pair in range(2):
                into, of = part * half + (2 * level + pair) * size, pair * rows // 2 + part * size
                copies.append(
                    pltpu.make_async_copy(
                        block.at[of : of + size, :],
                        a_ref.at[into : into + size, h * k : (h + 1) * k],
                        sems.at[len(copies)],
                    )
                )
    for copy in copies:
        copy.start()
    for copy in copies:
        copy.wait()
    wide = 512

    def column(n, carry):
        at = pl.ds(pl.multiple_of(n * wide, wide), wide)
        sums = sum(
            lax.dot_general(
                a_ref[:, h * k : (h + 1) * k], v_ref[at, :], (((1,), (1,)), ((), ())),
                preferred_element_type=jnp.float32,
            )
            for h, v_ref in enumerate(v_refs)
        )
        for part, out_ref in enumerate(out_refs):
            out_ref[:, :, at] = sums[part * half : (part + 1) * half].reshape(count, 2 * size, wide)
        return carry

    lax.fori_loop(0, v_refs[0].shape[0] // wide, column, 0)


def product(blocks, v, group, levels, sums):
    rows, k = blocks[0].shape
    count, size, ab = len(blocks) // 2, rows // 4, v[0].shape[0]
    place = pl.BlockSpec((count, 2 * size, ab), lambda i: (group, 0, 0))
    n = len(blocks) + 2
    return pl.pallas_call(
        functools.partial(product_kernel, size, count),
        grid=(1,),
        out_shape=[jax.ShapeDtypeStruct((levels, 2 * size, ab), jnp.float32)] * 2,
        in_specs=[pl.BlockSpec(memory_space=pl.ANY)] * (n + len(sums)),
        out_specs=[place] * 2,
        scratch_shapes=[
            pltpu.VMEM((count * rows, 2 * k), v[0].dtype),
            *[pltpu.VMEM(t.shape, t.dtype) for t in v],
            pltpu.SemaphoreType.DMA((2 + 4 * len(blocks),)),
        ],
        input_output_aliases={n + i: i for i in range(len(sums))},
        compiler_params=pltpu.CompilerParams(vmem_limit_bytes=28 << 20),
        cost_estimate=pl.CostEstimate(
            flops=4 * count * rows * ab * k,
            bytes_accessed=4 * count * rows * k + 4 * ab * k + 4 * count * rows * ab,
            transcendentals=0,
        ),
    )(*blocks, *v, *sums)


def mirror_kernel(tile_ref, lane_ref, sum_ref, out_ref):
    rows = sum_ref.shape[1]
    for t in range(64):
        twin = tile_ref[t]
        twin_column = pl.multiple_of((twin % 8) * TILE, TILE)
        own = sum_ref[t // 8, :, (t % 8) * TILE : (t % 8 + 1) * TILE]
        other = sum_ref[twin // 8, :, pl.ds(twin_column, TILE)]
        lanes = jnp.broadcast_to(lane_ref[t : t + 1, :], (rows, TILE))
        other = jnp.take_along_axis(other, lanes, axis=1)
        out_ref[t // 8, :, (t % 8) * TILE : (t % 8 + 1) * TILE] = (own - other).astype(out_ref.dtype)


def antisymmetrize(sums, mirror_rows):
    tiles = mirror_rows.reshape(-1, TILE)
    twin = tiles[:, 0] // TILE
    lanes = tiles % TILE
    return pl.pallas_call(
        mirror_kernel,
        out_shape=jax.ShapeDtypeStruct(sums.shape, jnp.bfloat16),
        in_specs=[
            pl.BlockSpec(memory_space=pltpu.SMEM),
            pl.BlockSpec(memory_space=pltpu.VMEM),
            pl.BlockSpec(memory_space=pltpu.VMEM),
        ],
        out_specs=pl.BlockSpec(memory_space=pltpu.VMEM),
    )(twin, lanes, sums)


def shards(levels, a, v, sym_rows, sym_cols, mirror_rows):
    z, y, x, c = (lax.axis_index(n) for n in "zyxc")
    ab, k = v.shape
    row_sym = jnp.repeat(sym_rows, TILE)

    def allowed(values, symmetry):
        col_sym = jnp.repeat(symmetry, TILE)
        return jnp.where(row_sym[:, None] == col_sym[None, :], values, jnp.zeros((), values.dtype))

    over = functools.partial(lax.ppermute, axis_name="c", perm=SWAP)
    v_over, sym_over = over(v), over(sym_cols)

    rows = a.shape[0] // 4
    size = rows // 2
    quads = a.reshape(2, 2, rows, k)
    mine, theirs = pick(quads, c, 1), pick(quads, 1 - c, 1)
    swapped = over(theirs)
    both = (allowed(v, sym_cols), allowed(v_over, sym_over))

    middle = levels // 2
    at_home = [t.reshape(2 * rows, k) for t in (mine, theirs)]
    moving = {(h, d): at_home[h] for h in range(2) for d in (1, -1)}
    blocks = [{0: t.reshape(2 * rows, k)} for t in (mine, swapped)]
    near = [r % levels for r in range(-2, 2)]
    far = [r % levels for r in range(2, levels - 2)]
    gathered = lambda group: [blocks[h][r] for r in group for h in range(2)]
    sums = ()
    for s in range(1, middle + 1):
        for h in range(2):
            ways = (1, -1) if s < middle else (1 - 2 * h,)
            if h and s == 3:
                sums = product(gathered(near), both, 0, levels, sums)
            for d in ways:
                if h and s == 1:
                    got = lax.ppermute(moving[h, d], ("z", "c"), cross(levels, d))
                else:
                    got = lax.ppermute(moving[h, d], "z", shift(levels, d))
                moving[h, d] = blocks[h][-s * d % levels] = got
    sums = product(gathered(far), both, 1, levels, sums)

    first = sums[0].reshape(4, 2, 2, size, ab)

    def parity(at):
        return (at // 2 - z) % 2

    def of_x(o):
        at = (x + o) % 4
        piece = lax.dynamic_slice(first, (0, parity(at), at % 2, 0, 0), (4, 1, 1, size, ab))
        return piece.reshape(4, size, ab)

    summed = scatter_ring(of_x, "x", True)
    turn = (x // 2 - z - parity(x)) // 2 + 1
    first = scatter_ring(lambda o: pick(summed, (y + o + turn) % 4, 0), "y", False)

    second = sums[1].reshape(levels, 2, size, ab)

    def of_y(o):
        at = 2 * (y + o) - z + 2
        return jnp.concatenate([pick(second, (at + i) % levels, 0) for i in range(2)])

    summed_y = scatter_ring(of_y, "y", True)
    second = scatter_ring(lambda o: pick(summed_y, (x + o) % 4, 0), "x", False)
    sums = jnp.concatenate([first, second], axis=0)

    share = rows // levels
    spread = lax.all_to_all(sums.reshape(levels, share, ab), "z", 0, 0)
    result = antisymmetrize(spread, mirror_rows)
    return lax.all_to_all(result, "z", 0, 0).reshape(rows, ab)


def solution(mesh):
    levels = mesh.shape["pair"]
    grid = Mesh(mesh.devices.reshape(levels, 4, 4, 2), ("z", "y", "x", "c"))
    plane = ("y", "x", "c")
    return jax.shard_map(
        functools.partial(shards, levels),
        mesh=grid,
        in_specs=(P("z", plane), P("z", plane), P("z"), P(plane), P()),
        out_specs=P(plane, "z"),
        check_vma=False,
    )
```

```python
import functools

import jax
import jax.numpy as jnp
from jax import lax
from jax.experimental import pallas as pl
from jax.experimental.pallas import tpu as pltpu
from jax.sharding import Mesh, PartitionSpec as P


TILE = 128
SWAP = ((0, 1), (1, 0))


def shift(n, d):
    return [(i, (i + d) % n) for i in range(n)]


def cross(n, d):
    return [(2 * i + c, 2 * ((i + d) % n) + 1 - c) for i in range(n) for c in range(2)]


def pick(array, index, axis):
    return lax.dynamic_index_in_dim(array, index, axis, keepdims=False)


def scatter_ring(part, axis, early):
    far = part(2)
    half = far.shape[0] // 2
    rest = [(0, 0)] * (far.ndim - 1)
    send_up = functools.partial(lax.ppermute, axis_name=axis, perm=shift(4, 1))
    send_down = functools.partial(lax.ppermute, axis_name=axis, perm=shift(4, -1))
    from_up = send_up(far[:half])
    from_down = send_down(far[half:])
    up, down = part(1), part(3)
    if not early:
        up = send_up(up + jnp.pad(from_up, [(0, half), *rest]))
        down = send_down(down + jnp.pad(from_down, [(half, 0), *rest]))
        return part(0) + up + down
    up_now = send_up(up[half:])
    down_now = send_down(down[:half])
    up = send_up(up[:half] + from_up)
    down = send_down(down[half:] + from_down)
    return (
        part(0)
        + jnp.pad(up + down_now, [(0, half), *rest])
        + jnp.pad(down + up_now, [(half, 0), *rest])
    )


def product_kernel(size, count, *refs):
    blocks, given = refs[: 2 * count], refs[2 * count : 2 * count + 2]
    *out_refs, a_ref, v_own, v_other, sems = refs[-6:]
    v_refs = (v_own, v_other)
    rows, k = blocks[0].shape
    half = 2 * size * count
    copies = [pltpu.make_async_copy(src, dst, sems.at[i]) for i, (src, dst) in enumerate(zip(given, v_refs))]
    for i, block in enumerate(blocks):
        level, h = divmod(i, 2)
        for part in range(2):
            for pair in range(2):
                into, of = part * half + (2 * level + pair) * size, pair * rows // 2 + part * size
                copies.append(
                    pltpu.make_async_copy(
                        block.at[of : of + size, :],
                        a_ref.at[into : into + size, h * k : (h + 1) * k],
                        sems.at[len(copies)],
                    )
                )
    for copy in copies:
        copy.start()
    for copy in copies:
        copy.wait()
    wide = 512

    def column(n, carry):
        at = pl.ds(pl.multiple_of(n * wide, wide), wide)
        sums = sum(
            lax.dot_general(
                a_ref[:, h * k : (h + 1) * k], v_ref[at, :], (((1,), (1,)), ((), ())),
                preferred_element_type=jnp.float32,
            )
            for h, v_ref in enumerate(v_refs)
        )
        for part, out_ref in enumerate(out_refs):
            out_ref[:, :, at] = sums[part * half : (part + 1) * half].reshape(count, 2 * size, wide)
        return carry

    lax.fori_loop(0, v_refs[0].shape[0] // wide, column, 0)


def product(blocks, v, group, levels, sums):
    rows, k = blocks[0].shape
    count, size, ab = len(blocks) // 2, rows // 4, v[0].shape[0]
    place = pl.BlockSpec((count, 2 * size, ab), lambda i: (group, 0, 0))
    n = len(blocks) + 2
    return pl.pallas_call(
        functools.partial(product_kernel, size, count),
        grid=(1,),
        out_shape=[jax.ShapeDtypeStruct((levels, 2 * size, ab), jnp.float32)] * 2,
        in_specs=[pl.BlockSpec(memory_space=pl.ANY)] * (n + len(sums)),
        out_specs=[place] * 2,
        scratch_shapes=[
            pltpu.VMEM((count * rows, 2 * k), v[0].dtype),
            *[pltpu.VMEM(t.shape, t.dtype) for t in v],
            pltpu.SemaphoreType.DMA((2 + 4 * len(blocks),)),
        ],
        input_output_aliases={n + i: i for i in range(len(sums))},
        compiler_params=pltpu.CompilerParams(vmem_limit_bytes=28 << 20),
        cost_estimate=pl.CostEstimate(
            flops=4 * count * rows * ab * k,
            bytes_accessed=4 * count * rows * k + 4 * ab * k + 4 * count * rows * ab,
            transcendentals=0,
        ),
    )(*blocks, *v, *sums)


def mirror_kernel(tile_ref, lane_ref, given_ref, out_ref, sum_ref, sem):
    copy = pltpu.make_async_copy(given_ref, sum_ref, sem)
    copy.start()
    copy.wait()
    rows = sum_ref.shape[1]
    for t in range(64):
        twin = tile_ref[t]
        twin_column = pl.multiple_of((twin % 8) * TILE, TILE)
        own = sum_ref[t // 8, :, (t % 8) * TILE : (t % 8 + 1) * TILE]
        other = sum_ref[twin // 8, :, pl.ds(twin_column, TILE)]
        lanes = jnp.broadcast_to(lane_ref[t : t + 1, :], (rows, TILE))
        other = jnp.take_along_axis(other, lanes, axis=1)
        out_ref[t // 8, :, (t % 8) * TILE : (t % 8 + 1) * TILE] = (own - other).astype(out_ref.dtype)


def antisymmetrize(sums, mirror_rows):
    tiles = mirror_rows.reshape(-1, TILE)
    twin = tiles[:, 0] // TILE
    lanes = tiles % TILE
    return pl.pallas_call(
        mirror_kernel,
        out_shape=jax.ShapeDtypeStruct(sums.shape, jnp.bfloat16),
        in_specs=[
            pl.BlockSpec(memory_space=pltpu.SMEM),
            pl.BlockSpec(memory_space=pltpu.VMEM),
            pl.BlockSpec(memory_space=pl.ANY),
        ],
        out_specs=pl.BlockSpec(memory_space=pltpu.VMEM),
        scratch_shapes=[pltpu.VMEM(sums.shape, sums.dtype), pltpu.SemaphoreType.DMA],
        compiler_params=pltpu.CompilerParams(vmem_limit_bytes=8 << 20),
    )(twin, lanes, sums)


def in_layer(levels, *args):
    return shards(levels, *args)


def shards(levels, a, v, sym_rows, sym_cols, mirror_rows):
    z, y, x, c = (lax.axis_index(n) for n in "zyxc")
    ab, k = v.shape
    row_sym = jnp.repeat(sym_rows, TILE)

    def allowed(values, symmetry):
        col_sym = jnp.repeat(symmetry, TILE)
        return jnp.where(row_sym[:, None] == col_sym[None, :], values, jnp.zeros((), values.dtype))

    over = functools.partial(lax.ppermute, axis_name="c", perm=SWAP)
    v_over, sym_over = over(v), over(sym_cols)

    rows = a.shape[0] // 4
    size = rows // 2
    quads = a.reshape(2, 2, rows, k)
    mine, theirs = pick(quads, c, 1), pick(quads, 1 - c, 1)
    swapped = over(theirs)
    both = (allowed(v, sym_cols), allowed(v_over, sym_over))

    middle = levels // 2
    at_home = [t.reshape(2 * rows, k) for t in (mine, theirs)]
    moving = {(h, d): at_home[h] for h in range(2) for d in (1, -1)}
    blocks = [{0: t.reshape(2 * rows, k)} for t in (mine, swapped)]
    near = [r % levels for r in range(-2, 2)]
    far = [r % levels for r in range(2, levels - 2)]
    gathered = lambda group: [blocks[h][r] for r in group for h in range(2)]
    sums = ()
    for s in range(1, middle + 1):
        for h in range(2):
            ways = (1, -1) if s < middle else (1 - 2 * h,)
            if h and s == 3:
                sums = product(gathered(near), both, 0, levels, sums)
            for d in ways:
                if h and s == 1:
                    got = lax.ppermute(moving[h, d], ("z", "c"), cross(levels, d))
                else:
                    got = lax.ppermute(moving[h, d], "z", shift(levels, d))
                moving[h, d] = blocks[h][-s * d % levels] = got
    sums = product(gathered(far), both, 1, levels, sums)

    first = sums[0].reshape(4, 2, 2, size, ab)

    def parity(at):
        return (at // 2 - z) % 2

    def of_x(o):
        at = (x + o) % 4
        piece = lax.dynamic_slice(first, (0, parity(at), at % 2, 0, 0), (4, 1, 1, size, ab))
        return piece.reshape(4, size, ab)

    summed = scatter_ring(of_x, "x", True)
    turn = (x // 2 - z - parity(x)) // 2 + 1
    first = scatter_ring(lambda o: pick(summed, (y + o + turn) % 4, 0), "y", False)

    second = sums[1].reshape(levels, 2, size, ab)

    def of_y(o):
        at = 2 * (y + o) - z + 2
        return jnp.concatenate([pick(second, (at + i) % levels, 0) for i in range(2)])

    summed_y = scatter_ring(of_y, "y", True)
    second = scatter_ring(lambda o: pick(summed_y, (x + o) % 4, 0), "x", False)
    sums = jnp.concatenate([first, second], axis=0)

    share = rows // levels
    spread = lax.all_to_all(sums.reshape(levels, share, ab), "z", 0, 0)
    result = antisymmetrize(spread, mirror_rows)
    return lax.all_to_all(result, "z", 0, 0).reshape(rows, ab)


def solution(mesh):
    levels = mesh.shape["pair"]
    grid = Mesh(mesh.devices.reshape(levels, 4, 4, 2), ("z", "y", "x", "c"))
    plane = ("y", "x", "c")
    return jax.shard_map(
        functools.partial(in_layer, levels),
        mesh=grid,
        in_specs=(P("z", plane), P("z", plane), P("z"), P(plane), P()),
        out_specs=P(plane, "z"),
        check_vma=False,
    )
```

```python
import functools

import jax
import jax.numpy as jnp
from jax import lax
from jax.experimental import pallas as pl
from jax.experimental.pallas import tpu as pltpu
from jax.sharding import Mesh, PartitionSpec as P


TILE = 128
SWAP = ((0, 1), (1, 0))


def shift(n, d):
    return [(i, (i + d) % n) for i in range(n)]


def cross(n, d):
    return [(2 * i + c, 2 * ((i + d) % n) + 1 - c) for i in range(n) for c in range(2)]


def pick(array, index, axis):
    return lax.dynamic_index_in_dim(array, index, axis, keepdims=False)


def scatter_ring(part, axis, early):
    far = part(2)
    half = far.shape[0] // 2
    rest = [(0, 0)] * (far.ndim - 1)
    send_up = functools.partial(lax.ppermute, axis_name=axis, perm=shift(4, 1))
    send_down = functools.partial(lax.ppermute, axis_name=axis, perm=shift(4, -1))
    from_up = send_up(far[:half])
    from_down = send_down(far[half:])
    up, down = part(1), part(3)
    if not early:
        up = send_up(up + jnp.pad(from_up, [(0, half), *rest]))
        down = send_down(down + jnp.pad(from_down, [(half, 0), *rest]))
        return part(0) + up + down
    up_now = send_up(up[half:])
    down_now = send_down(down[:half])
    up = send_up(up[:half] + from_up)
    down = send_down(down[half:] + from_down)
    return (
        part(0)
        + jnp.pad(up + down_now, [(0, half), *rest])
        + jnp.pad(down + up_now, [(half, 0), *rest])
    )


def product_kernel(size, count, *refs):
    blocks, given = refs[: 2 * count], refs[2 * count : 2 * count + 2]
    *out_refs, a_ref, v_own, v_other, sems = refs[-6:]
    v_refs = (v_own, v_other)
    rows, k = blocks[0].shape
    half = 2 * size * count
    copies = [pltpu.make_async_copy(src, dst, sems.at[i]) for i, (src, dst) in enumerate(zip(given, v_refs))]
    for i, block in enumerate(blocks):
        level, h = divmod(i, 2)
        for part in range(2):
            for pair in range(2):
                into, of = part * half + (2 * level + pair) * size, pair * rows // 2 + part * size
                copies.append(
                    pltpu.make_async_copy(
                        block.at[of : of + size, :],
                        a_ref.at[into : into + size, h * k : (h + 1) * k],
                        sems.at[len(copies)],
                    )
                )
    for copy in copies:
        copy.start()
    for copy in copies:
        copy.wait()
    wide = 512

    def column(n, carry):
        at = pl.ds(pl.multiple_of(n * wide, wide), wide)
        sums = sum(
            lax.dot_general(
                a_ref[:, h * k : (h + 1) * k], v_ref[at, :], (((1,), (1,)), ((), ())),
                preferred_element_type=jnp.float32,
            )
            for h, v_ref in enumerate(v_refs)
        )
        for part, out_ref in enumerate(out_refs):
            out_ref[:, :, at] = sums[part * half : (part + 1) * half].reshape(count, 2 * size, wide)
        return carry

    lax.fori_loop(0, v_refs[0].shape[0] // wide, column, 0)


def product(blocks, v, group, levels, sums):
    rows, k = blocks[0].shape
    count, size, ab = len(blocks) // 2, rows // 4, v[0].shape[0]
    place = pl.BlockSpec((count, 2 * size, ab), lambda i: (group, 0, 0))
    n = len(blocks) + 2
    return pl.pallas_call(
        functools.partial(product_kernel, size, count),
        grid=(1,),
        out_shape=[
            jax.ShapeDtypeStruct((levels, 2 * size, ab), jnp.float32),
            pltpu.HBM((levels, 2 * size, ab), jnp.float32),
        ],
        in_specs=[pl.BlockSpec(memory_space=pl.ANY)] * (n + len(sums)),
        out_specs=[place] * 2,
        scratch_shapes=[
            pltpu.VMEM((count * rows, 2 * k), v[0].dtype),
            *[pltpu.VMEM(t.shape, t.dtype) for t in v],
            pltpu.SemaphoreType.DMA((2 + 4 * len(blocks),)),
        ],
        input_output_aliases={n + i: i for i in range(len(sums))},
        compiler_params=pltpu.CompilerParams(vmem_limit_bytes=28 << 20),
        cost_estimate=pl.CostEstimate(
            flops=4 * count * rows * ab * k,
            bytes_accessed=4 * count * rows * k + 4 * ab * k + 4 * count * rows * ab,
            transcendentals=0,
        ),
    )(*blocks, *v, *sums)


def mirror_kernel(tile_ref, lane_ref, given_ref, out_ref, sum_ref, sem):
    copy = pltpu.make_async_copy(given_ref, sum_ref, sem)
    copy.start()
    copy.wait()
    rows = sum_ref.shape[1]
    for t in range(64):
        twin = tile_ref[t]
        twin_column = pl.multiple_of((twin % 8) * TILE, TILE)
        own = sum_ref[t // 8, :, (t % 8) * TILE : (t % 8 + 1) * TILE]
        other = sum_ref[twin // 8, :, pl.ds(twin_column, TILE)]
        lanes = jnp.broadcast_to(lane_ref[t : t + 1, :], (rows, TILE))
        other = jnp.take_along_axis(other, lanes, axis=1)
        out_ref[t // 8, :, (t % 8) * TILE : (t % 8 + 1) * TILE] = (own - other).astype(out_ref.dtype)


def antisymmetrize(sums, mirror_rows):
    tiles = mirror_rows.reshape(-1, TILE)
    twin = tiles[:, 0] // TILE
    lanes = tiles % TILE
    return pl.pallas_call(
        mirror_kernel,
        out_shape=jax.ShapeDtypeStruct(sums.shape, jnp.bfloat16),
        in_specs=[
            pl.BlockSpec(memory_space=pltpu.SMEM),
            pl.BlockSpec(memory_space=pltpu.VMEM),
            pl.BlockSpec(memory_space=pl.ANY),
        ],
        out_specs=pl.BlockSpec(memory_space=pltpu.VMEM),
        scratch_shapes=[pltpu.VMEM(sums.shape, sums.dtype), pltpu.SemaphoreType.DMA],
        compiler_params=pltpu.CompilerParams(vmem_limit_bytes=8 << 20),
    )(twin, lanes, sums)


def in_layer(levels, *args):
    return shards(levels, *args)


def shards(levels, a, v, sym_rows, sym_cols, mirror_rows):
    z, y, x, c = (lax.axis_index(n) for n in "zyxc")
    ab, k = v.shape
    row_sym = jnp.repeat(sym_rows, TILE)

    def allowed(values, symmetry):
        col_sym = jnp.repeat(symmetry, TILE)
        return jnp.where(row_sym[:, None] == col_sym[None, :], values, jnp.zeros((), values.dtype))

    over = functools.partial(lax.ppermute, axis_name="c", perm=SWAP)
    v_over, sym_over = over(v), over(sym_cols)

    rows = a.shape[0] // 4
    size = rows // 2
    quads = a.reshape(2, 2, rows, k)
    mine, theirs = pick(quads, c, 1), pick(quads, 1 - c, 1)
    swapped = over(theirs)
    both = (allowed(v, sym_cols), allowed(v_over, sym_over))

    middle = levels // 2
    at_home = [t.reshape(2 * rows, k) for t in (mine, theirs)]
    moving = {(h, d): at_home[h] for h in range(2) for d in (1, -1)}
    blocks = [{0: t.reshape(2 * rows, k)} for t in (mine, swapped)]
    near = [r % levels for r in range(-2, 2)]
    far = [r % levels for r in range(2, levels - 2)]
    gathered = lambda group: [blocks[h][r] for r in group for h in range(2)]
    sums = ()
    for s in range(1, middle + 1):
        for h in range(2):
            ways = (1, -1) if s < middle else (1 - 2 * h,)
            if h and s == 3:
                sums = product(gathered(near), both, 0, levels, sums)
            for d in ways:
                if h and s == 1:
                    got = lax.ppermute(moving[h, d], ("z", "c"), cross(levels, d))
                else:
                    got = lax.ppermute(moving[h, d], "z", shift(levels, d))
                moving[h, d] = blocks[h][-s * d % levels] = got
    sums = product(gathered(far), both, 1, levels, sums)

    first = sums[0].reshape(4, 2, 2, size, ab)

    def parity(at):
        return (at // 2 - z) % 2

    def of_x(o):
        at = (x + o) % 4
        piece = lax.dynamic_slice(first, (0, parity(at), at % 2, 0, 0), (4, 1, 1, size, ab))
        return piece.reshape(4, size, ab)

    summed = scatter_ring(of_x, "x", True)
    turn = (x // 2 - z - parity(x)) // 2 + 1
    first = scatter_ring(lambda o: pick(summed, (y + o + turn) % 4, 0), "y", False)

    second = sums[1].reshape(levels, 2, size, ab)

    def of_y(o):
        at = 2 * (y + o) - z + 2
        return jnp.concatenate([pick(second, (at + i) % levels, 0) for i in range(2)])

    summed_y = scatter_ring(of_y, "y", True)
    second = scatter_ring(lambda o: pick(summed_y, (x + o) % 4, 0), "x", False)
    sums = jnp.concatenate([first, second], axis=0)

    share = rows // levels
    spread = lax.all_to_all(sums.reshape(levels, share, ab), "z", 0, 0)
    result = antisymmetrize(spread, mirror_rows)
    return lax.all_to_all(result, "z", 0, 0).reshape(rows, ab)


def solution(mesh):
    levels = mesh.shape["pair"]
    grid = Mesh(mesh.devices.reshape(levels, 4, 4, 2), ("z", "y", "x", "c"))
    plane = ("y", "x", "c")
    return jax.shard_map(
        functools.partial(in_layer, levels),
        mesh=grid,
        in_specs=(P("z", plane), P("z", plane), P("z"), P(plane), P()),
        out_specs=P(plane, "z"),
        check_vma=False,
    )
```

```python
import functools

import jax
import jax.numpy as jnp
from jax import lax
from jax.experimental import pallas as pl
from jax.experimental.pallas import tpu as pltpu
from jax.sharding import Mesh, PartitionSpec as P


TILE = 128
SWAP = ((0, 1), (1, 0))


def shift(n, d):
    return [(i, (i + d) % n) for i in range(n)]


def cross(n, d):
    return [(2 * i + c, 2 * ((i + d) % n) + 1 - c) for i in range(n) for c in range(2)]


def pick(array, index, axis):
    return lax.dynamic_index_in_dim(array, index, axis, keepdims=False)


def scatter_ring(part, axis, early):
    far = part(2)
    half = far.shape[0] // 2
    rest = [(0, 0)] * (far.ndim - 1)
    send_up = functools.partial(lax.ppermute, axis_name=axis, perm=shift(4, 1))
    send_down = functools.partial(lax.ppermute, axis_name=axis, perm=shift(4, -1))
    from_up = send_up(far[:half])
    from_down = send_down(far[half:])
    up, down = part(1), part(3)
    if not early:
        up = send_up(up + jnp.pad(from_up, [(0, half), *rest]))
        down = send_down(down + jnp.pad(from_down, [(half, 0), *rest]))
        return part(0) + up + down
    up_now = send_up(up[half:])
    down_now = send_down(down[:half])
    up = send_up(up[:half] + from_up)
    down = send_down(down[half:] + from_down)
    return (
        part(0)
        + jnp.pad(up + down_now, [(0, half), *rest])
        + jnp.pad(down + up_now, [(half, 0), *rest])
    )


def product_kernel(size, count, *refs):
    blocks, given = refs[: 2 * count], refs[2 * count : 2 * count + 2]
    *out_refs, a_ref, v_own, v_other, sems = refs[-6:]
    v_refs = (v_own, v_other)
    rows, k = blocks[0].shape
    half = 2 * size * count
    copies = [pltpu.make_async_copy(src, dst, sems.at[i]) for i, (src, dst) in enumerate(zip(given, v_refs))]
    for i, block in enumerate(blocks):
        level, h = divmod(i, 2)
        for part in range(2):
            for pair in range(2):
                into, of = part * half + (2 * level + pair) * size, pair * rows // 2 + part * size
                copies.append(
                    pltpu.make_async_copy(
                        block.at[of : of + size, :],
                        a_ref.at[into : into + size, h * k : (h + 1) * k],
                        sems.at[len(copies)],
                    )
                )
    for copy in copies:
        copy.start()
    for copy in copies:
        copy.wait()
    wide = 512

    def column(n, carry):
        at = pl.ds(pl.multiple_of(n * wide, wide), wide)
        sums = sum(
            lax.dot_general(
                a_ref[:, h * k : (h + 1) * k], v_ref[at, :], (((1,), (1,)), ((), ())),
                preferred_element_type=jnp.float32,
            )
            for h, v_ref in enumerate(v_refs)
        )
        for part, out_ref in enumerate(out_refs):
            out_ref[:, :, at] = sums[part * half : (part + 1) * half].reshape(count, 2 * size, wide)
        return carry

    lax.fori_loop(0, v_refs[0].shape[0] // wide, column, 0)


def product(blocks, v, group, levels, sums):
    rows, k = blocks[0].shape
    count, size, ab = len(blocks) // 2, rows // 4, v[0].shape[0]
    place = pl.BlockSpec((count, 2 * size, ab), lambda i: (group, 0, 0))
    n = len(blocks) + 2
    return pl.pallas_call(
        functools.partial(product_kernel, size, count),
        grid=(1,),
        out_shape=[
            jax.ShapeDtypeStruct((levels, 2 * size, ab), jnp.float32),
            pltpu.HBM((levels, 2 * size, ab), jnp.float32),
        ],
        in_specs=[pl.BlockSpec(memory_space=pl.ANY)] * (n + len(sums)),
        out_specs=[place] * 2,
        scratch_shapes=[
            pltpu.VMEM((count * rows, 2 * k), v[0].dtype),
            *[pltpu.VMEM(t.shape, t.dtype) for t in v],
            pltpu.SemaphoreType.DMA((2 + 4 * len(blocks),)),
        ],
        input_output_aliases={n + i: i for i in range(len(sums))},
        compiler_params=pltpu.CompilerParams(vmem_limit_bytes=28 << 20),
        cost_estimate=pl.CostEstimate(
            flops=4 * count * rows * ab * k,
            bytes_accessed=4 * count * rows * k + 4 * ab * k + 4 * count * rows * ab,
            transcendentals=0,
        ),
    )(*blocks, *v, *sums)


def mirror_kernel(tile_ref, lane_ref, given_ref, out_ref, sum_ref, sem):
    copy = pltpu.make_async_copy(given_ref, sum_ref, sem)
    copy.start()
    copy.wait()
    rows = sum_ref.shape[1]
    for t in range(64):
        twin = tile_ref[t]
        twin_column = pl.multiple_of((twin % 8) * TILE, TILE)
        own = sum_ref[t // 8, :, (t % 8) * TILE : (t % 8 + 1) * TILE]
        other = sum_ref[twin // 8, :, pl.ds(twin_column, TILE)]
        lanes = jnp.broadcast_to(lane_ref[t : t + 1, :], (rows, TILE))
        other = jnp.take_along_axis(other, lanes, axis=1)
        out_ref[t // 8, :, (t % 8) * TILE : (t % 8 + 1) * TILE] = (own - other).astype(out_ref.dtype)


def antisymmetrize(sums, mirror_rows):
    tiles = mirror_rows.reshape(-1, TILE)
    twin = tiles[:, 0] // TILE
    lanes = tiles % TILE
    return pl.pallas_call(
        mirror_kernel,
        out_shape=jax.ShapeDtypeStruct(sums.shape, jnp.bfloat16),
        in_specs=[
            pl.BlockSpec(memory_space=pltpu.SMEM),
            pl.BlockSpec(memory_space=pltpu.VMEM),
            pl.BlockSpec(memory_space=pl.ANY),
        ],
        out_specs=pl.BlockSpec(memory_space=pltpu.VMEM),
        scratch_shapes=[pltpu.VMEM(sums.shape, sums.dtype), pltpu.SemaphoreType.DMA],
        compiler_params=pltpu.CompilerParams(vmem_limit_bytes=8 << 20),
    )(twin, lanes, sums)


def in_layer(levels, *args):
    return shards(levels, *args)


def shards(levels, a, v, sym_rows, sym_cols, mirror_rows):
    z, y, x, c = (lax.axis_index(n) for n in "zyxc")
    ab, k = v.shape
    row_sym = jnp.repeat(sym_rows, TILE)

    def allowed(values, symmetry):
        col_sym = jnp.repeat(symmetry, TILE)
        return jnp.where(row_sym[:, None] == col_sym[None, :], values, jnp.zeros((), values.dtype))

    over = functools.partial(lax.ppermute, axis_name="c", perm=SWAP)
    v_over, sym_over = over(v), over(sym_cols)

    rows = a.shape[0] // 4
    size = rows // 2
    quads = a.reshape(2, 2, rows, k)
    mine, theirs = pick(quads, c, 1), pick(quads, 1 - c, 1)
    swapped = over(theirs)
    both = (allowed(v, sym_cols), allowed(v_over, sym_over))

    middle = levels // 2
    at_home = [t.reshape(2 * rows, k) for t in (mine, theirs)]
    moving = {(h, d): at_home[h] for h in range(2) for d in (1, -1)}
    blocks = [{0: t.reshape(2 * rows, k)} for t in (mine, swapped)]
    near = [r % levels for r in range(-2, 2)]
    far = [r % levels for r in range(2, levels - 2)]
    gathered = lambda group: [blocks[h][r] for r in group for h in range(2)]
    sums = ()
    for s in range(1, middle + 1):
        for h in range(2):
            ways = (1, -1) if s < middle else (1 - 2 * h,)
            if h and s == 3:
                sums = product(gathered(near), both, 0, levels, sums)
            for d in ways:
                if h and s == 1:
                    got = lax.ppermute(moving[h, d], ("z", "c"), cross(levels, d))
                else:
                    got = lax.ppermute(moving[h, d], "z", shift(levels, d))
                moving[h, d] = blocks[h][-s * d % levels] = got
    sums = product(gathered(far), both, 1, levels, sums)

    first = sums[0].reshape(4, 2, 2, size, ab)

    def parity(at):
        return (at // 2 - z) % 2

    def of_x(o):
        at = (x + o) % 4
        piece = lax.dynamic_slice(first, (0, parity(at), at % 2, 0, 0), (4, 1, 1, size, ab))
        return piece.reshape(4, size, ab)

    summed = scatter_ring(of_x, "x", True)
    turn = (x // 2 - z - parity(x)) // 2 + 1
    first = scatter_ring(lambda o: pick(summed, (y + o + turn) % 4, 0), "y", False)

    second = sums[1].reshape(levels, 2, size, ab)

    def of_y(o):
        at = 2 * (y + o) - z + 2
        return jnp.concatenate([pick(second, (at + i) % levels, 0) for i in range(2)])

    summed_y = scatter_ring(of_y, "y", True)
    second = scatter_ring(lambda o: pick(summed_y, (x + o) % 4, 0), "x", False)
    sums = jnp.concatenate([first, second], axis=0)

    share = rows // levels
    grouped = (levels, share // 4, 4, ab)
    spread = lax.all_to_all(sums.reshape(grouped), "z", 0, 0)
    result = antisymmetrize(spread.reshape(levels, share, ab), mirror_rows)
    return lax.all_to_all(result.reshape(grouped), "z", 0, 0).reshape(rows, ab)


def solution(mesh):
    levels = mesh.shape["pair"]
    grid = Mesh(mesh.devices.reshape(levels, 4, 4, 2), ("z", "y", "x", "c"))
    plane = ("y", "x", "c")
    return jax.shard_map(
        functools.partial(in_layer, levels),
        mesh=grid,
        in_specs=(P("z", plane), P("z", plane), P("z"), P(plane), P()),
        out_specs=P(plane, "z"),
        check_vma=False,
    )
```

```python
import functools

import jax
import jax.numpy as jnp
from jax import lax
from jax.experimental import pallas as pl
from jax.experimental.pallas import tpu as pltpu
from jax.sharding import Mesh, PartitionSpec as P


TILE = 128
SWAP = ((0, 1), (1, 0))


def shift(n, d):
    return [(i, (i + d) % n) for i in range(n)]


def cross(n, d):
    return [(2 * i + c, 2 * ((i + d) % n) + 1 - c) for i in range(n) for c in range(2)]


def pick(array, index, axis):
    return lax.dynamic_index_in_dim(array, index, axis, keepdims=False)


def scatter_ring(part, axis, early):
    far = part(2)
    half = far.shape[0] // 2
    rest = [(0, 0)] * (far.ndim - 1)
    send_up = functools.partial(lax.ppermute, axis_name=axis, perm=shift(4, 1))
    send_down = functools.partial(lax.ppermute, axis_name=axis, perm=shift(4, -1))
    from_up = send_up(far[:half])
    from_down = send_down(far[half:])
    up, down = part(1), part(3)
    if not early:
        up = send_up(up + jnp.pad(from_up, [(0, half), *rest]))
        down = send_down(down + jnp.pad(from_down, [(half, 0), *rest]))
        return part(0) + up + down
    up_now = send_up(up[half:])
    down_now = send_down(down[:half])
    up = send_up(up[:half] + from_up)
    down = send_down(down[half:] + from_down)
    return (
        part(0)
        + jnp.pad(up + down_now, [(0, half), *rest])
        + jnp.pad(down + up_now, [(half, 0), *rest])
    )


def product_kernel(size, count, *refs):
    blocks, v_refs = refs[: 2 * count], refs[2 * count : 2 * count + 2]
    *out_refs, a_ref, sems = refs[-4:]
    rows, k = blocks[0].shape
    half = 2 * size * count

    @pl.when(pl.program_id(0) == 0)
    def _():
        copies = []
        for i, block in enumerate(blocks):
            level, h = divmod(i, 2)
            for part in range(2):
                for pair in range(2):
                    into, of = part * half + (2 * level + pair) * size, pair * rows // 2 + part * size
                    copies.append(
                        pltpu.make_async_copy(
                            block.at[of : of + size, :],
                            a_ref.at[into : into + size, h * k : (h + 1) * k],
                            sems.at[len(copies)],
                        )
                    )
        for copy in copies:
            copy.start()
        for copy in copies:
            copy.wait()

    sums = sum(
        lax.dot_general(
            a_ref[:, h * k : (h + 1) * k], v_ref[...], (((1,), (1,)), ((), ())),
            preferred_element_type=jnp.float32,
        )
        for h, v_ref in enumerate(v_refs)
    )
    for part, out_ref in enumerate(out_refs):
        out_ref[...] = sums[part * half : (part + 1) * half].reshape(out_ref.shape)


def product(blocks, v, group, levels, sums):
    rows, k = blocks[0].shape
    count, size, ab = len(blocks) // 2, rows // 4, v[0].shape[0]
    wide = ab // 2
    place = pl.BlockSpec((count, 2 * size, wide), lambda i: (group, 0, i))
    columns = pl.BlockSpec((wide, k), lambda i: (i, 0))
    stay = pl.BlockSpec(memory_space=pl.ANY)
    n = len(blocks) + 2
    return pl.pallas_call(
        functools.partial(product_kernel, size, count),
        grid=(2,),
        out_shape=[
            jax.ShapeDtypeStruct((levels, 2 * size, ab), jnp.float32),
            pltpu.HBM((levels, 2 * size, ab), jnp.float32),
        ],
        in_specs=[stay] * len(blocks) + [columns] * 2 + [stay] * len(sums),
        out_specs=[place] * 2,
        scratch_shapes=[
            pltpu.VMEM((count * rows, 2 * k), v[0].dtype),
            pltpu.SemaphoreType.DMA((4 * len(blocks),)),
        ],
        input_output_aliases={n + i: i for i in range(len(sums))},
        compiler_params=pltpu.CompilerParams(vmem_limit_bytes=28 << 20),
        cost_estimate=pl.CostEstimate(
            flops=4 * count * rows * ab * k,
            bytes_accessed=4 * count * rows * k + 4 * ab * k + 4 * count * rows * ab,
            transcendentals=0,
        ),
    )(*blocks, *v, *sums)


def mirror_kernel(tile_ref, lane_ref, given_ref, out_ref, sum_ref, sem):
    copy = pltpu.make_async_copy(given_ref, sum_ref, sem)
    copy.start()
    copy.wait()
    rows = sum_ref.shape[1]
    for t in range(64):
        twin = tile_ref[t]
        twin_column = pl.multiple_of((twin % 8) * TILE, TILE)
        own = sum_ref[t // 8, :, (t % 8) * TILE : (t % 8 + 1) * TILE]
        other = sum_ref[twin // 8, :, pl.ds(twin_column, TILE)]
        lanes = jnp.broadcast_to(lane_ref[t : t + 1, :], (rows, TILE))
        other = jnp.take_along_axis(other, lanes, axis=1)
        out_ref[t // 8, :, (t % 8) * TILE : (t % 8 + 1) * TILE] = (own - other).astype(out_ref.dtype)


def antisymmetrize(sums, mirror_rows):
    tiles = mirror_rows.reshape(-1, TILE)
    twin = tiles[:, 0] // TILE
    lanes = tiles % TILE
    return pl.pallas_call(
        mirror_kernel,
        out_shape=jax.ShapeDtypeStruct(sums.shape, jnp.bfloat16),
        in_specs=[
            pl.BlockSpec(memory_space=pltpu.SMEM),
            pl.BlockSpec(memory_space=pltpu.VMEM),
            pl.BlockSpec(memory_space=pl.ANY),
        ],
        out_specs=pl.BlockSpec(memory_space=pltpu.VMEM),
        scratch_shapes=[pltpu.VMEM(sums.shape, sums.dtype), pltpu.SemaphoreType.DMA],
        compiler_params=pltpu.CompilerParams(vmem_limit_bytes=8 << 20),
    )(twin, lanes, sums)


def in_layer(levels, *args):
    return shards(levels, *args)


def shards(levels, a, v, sym_rows, sym_cols, mirror_rows):
    z, y, x, c = (lax.axis_index(n) for n in "zyxc")
    ab, k = v.shape
    row_sym = jnp.repeat(sym_rows, TILE)

    def allowed(values, symmetry):
        col_sym = jnp.repeat(symmetry, TILE)
        return jnp.where(row_sym[:, None] == col_sym[None, :], values, jnp.zeros((), values.dtype))

    over = functools.partial(lax.ppermute, axis_name="c", perm=SWAP)
    v_over, sym_over = over(v), over(sym_cols)

    rows = a.shape[0] // 4
    size = rows // 2
    quads = a.reshape(2, 2, rows, k)
    mine, theirs = pick(quads, c, 1), pick(quads, 1 - c, 1)
    swapped = over(theirs)
    both = (allowed(v, sym_cols), allowed(v_over, sym_over))

    middle = levels // 2
    at_home = [t.reshape(2 * rows, k) for t in (mine, theirs)]
    moving = {(h, d): at_home[h] for h in range(2) for d in (1, -1)}
    blocks = [{0: t.reshape(2 * rows, k)} for t in (mine, swapped)]
    near = [r % levels for r in range(-2, 2)]
    far = [r % levels for r in range(2, levels - 2)]
    gathered = lambda group: [blocks[h][r] for r in group for h in range(2)]
    sums = ()
    for s in range(1, middle + 1):
        for h in range(2):
            ways = (1, -1) if s < middle else (1 - 2 * h,)
            if h and s == 3:
                sums = product(gathered(near), both, 0, levels, sums)
            for d in ways:
                if h and s == 1:
                    got = lax.ppermute(moving[h, d], ("z", "c"), cross(levels, d))
                else:
                    got = lax.ppermute(moving[h, d], "z", shift(levels, d))
                moving[h, d] = blocks[h][-s * d % levels] = got
    sums = product(gathered(far), both, 1, levels, sums)

    first = sums[0].reshape(4, 2, 2, size, ab)

    def parity(at):
        return (at // 2 - z) % 2

    def of_x(o):
        at = (x + o) % 4
        piece = lax.dynamic_slice(first, (0, parity(at), at % 2, 0, 0), (4, 1, 1, size, ab))
        return piece.reshape(4, size, ab)

    summed = scatter_ring(of_x, "x", True)
    turn = (x // 2 - z - parity(x)) // 2 + 1
    first = scatter_ring(lambda o: pick(summed, (y + o + turn) % 4, 0), "y", False)

    second = sums[1].reshape(levels, 2, size, ab)

    def of_y(o):
        at = 2 * (y + o) - z + 2
        return jnp.concatenate([pick(second, (at + i) % levels, 0) for i in range(2)])

    summed_y = scatter_ring(of_y, "y", True)
    second = scatter_ring(lambda o: pick(summed_y, (x + o) % 4, 0), "x", False)
    sums = jnp.concatenate([first, second], axis=0)

    share = rows // levels
    grouped = (levels, share // 4, 4, ab)
    spread = lax.all_to_all(sums.reshape(grouped), "z", 0, 0)
    result = antisymmetrize(spread.reshape(levels, share, ab), mirror_rows)
    return lax.all_to_all(result.reshape(grouped), "z", 0, 0).reshape(rows, ab)


def solution(mesh):
    levels = mesh.shape["pair"]
    grid = Mesh(mesh.devices.reshape(levels, 4, 4, 2), ("z", "y", "x", "c"))
    plane = ("y", "x", "c")
    return jax.shard_map(
        functools.partial(in_layer, levels),
        mesh=grid,
        in_specs=(P("z", plane), P("z", plane), P("z"), P(plane), P()),
        out_specs=P(plane, "z"),
        check_vma=False,
    )
```
